32 devices in a mesh: ctx: 4 (over z), rec: 8 (over y, x, core).
Axes of the slice: x: 2, y: 2, z: 4, core: 2. Of those that a mesh axis runs over, the one named last changes fastest.
Arguments:
- queries: bfloat16 [8, 1024, 1280], P('rec', 'ctx'), may hold values from -24 to 24
- video_keys: bfloat16 [8, 512, 1280], P('rec', 'ctx'), may hold values from -24 to 24
- video_values: bfloat16 [8, 512, 1280], P('rec', 'ctx'), may hold values from -6 to 6
- out_weight: bfloat16 [1280, 1280], replicated, may hold values from -0.15625 to 0.15625
- gate_logit: float32 [1], replicated, may hold values from 0.3 to 1.2
- row_grads: bfloat16 [16384, 1280], P(('ctx', 'rec')), may hold values from -6 to 6
- dest_device: int32 [16384], P(('ctx', 'rec')), may hold values from 0 to 31, as said below
- dest_row: int32 [16384], P(('ctx', 'rec')), may hold values from 0 to 255, as said below
- live_count: int32 [32], P(('ctx', 'rec')), may hold values from 0 to 512, as said below
Outputs:
- query_grads: bfloat16 [16384, 1280], P(('ctx', 'rec'))
- key_grads: bfloat16 [8, 512, 1280], P('rec', 'ctx')
- value_grads: bfloat16 [8, 512, 1280], P('rec', 'ctx')
- weight_grads: float32 [1280, 1280], P(('ctx', 'rec'))
- gate_grad: float32 [1], replicated
The draws below stay inside these ranges and needn't reach their ends.
Inputs may be any that keep to these rules, and one draw needn't show every extreme that they name: `dest_device`: for the live slots of all devices together, each pair of owner device and audio row appears exactly once; the live slots of one device name one owner at most 16 times, and some device names each owner exactly 16 times. Slots that are not live hold 0. `dest_row`: slots that are not live hold 0. `live_count`: the live slots of a device are its first ones; the counts sum to 8192, and the largest is exactly 512.
All inputs are finite; a program needn't handle non-finite values.
Results may differ from the reference program's by a relative error of at most 0.012.
The reference program's roundings to bfloat16 on the way count: a program that leaves them out, or rounds other values in their place, can miss the bound.
Values may be sent and summed in bfloat16 or wider, within the bound.
No kernel may reach another device: no remote copies, remote signals or barrier semaphores. Data moves between devices by JAX's collectives and lax.ppermute only.
A program may use at most 192 MiB of HBM per device.

```python
from functools import partial
import jax
import jax.numpy as jnp
from jax import lax

D = 1280
HEADS = 20
HEAD_DIM = 64
AUD_DEV = 256
RECS = 8
AUDIO = 1024
VIDEO = 512
LLM_DEV = 512
LLM_ROWS = 16384
N_CTX = 4
N_REC = 8
DEVICES = 32


def draw_queries(key, part):
    values = jnp.clip(jax.random.normal(jax.random.fold_in(key, 1), (RECS, AUDIO, D), jnp.float32), -6.0, 6.0)
    return values.astype(jnp.bfloat16)


def draw_video_keys(key, part):
    values = jnp.clip(jax.random.normal(jax.random.fold_in(key, 3), (RECS, VIDEO, D), jnp.float32), -6.0, 6.0)
    return values.astype(jnp.bfloat16)


def route_tables(key):
    device_total = DEVICES
    pair_cap = 2 * AUD_DEV // DEVICES
    half_cap = pair_cap // 2
    slot_total = device_total * pair_cap
    keys = jax.random.split(key, 5)
    order = jax.random.permutation(keys[0], device_total).astype(jnp.int32)
    position = jnp.argsort(order).astype(jnp.int32)
    pair_id = position // 2
    sign_of = 1 - 2 * (position % 2)
    heavy = jax.random.randint(keys[1], (device_total // 2,), 0, half_cap + 1).at[0].set(half_cap)
    jitter = jax.random.randint(keys[2], (device_total // 2, device_total), -1, 2)
    extra = jnp.clip(heavy[:, None] + jitter, 0, half_cap).at[0].set(half_cap)
    counts = half_cap + sign_of[:, None] * extra[pair_id]
    candidate = jnp.arange(slot_total, dtype=jnp.int32)
    cand_dest = candidate // pair_cap
    cand_turn = candidate % pair_cap
    alive = cand_turn[None, :] < counts[:, cand_dest]
    shuffle = jax.vmap(partial(jax.random.permutation, x=slot_total))(jax.random.split(keys[3], device_total))
    sort_key = shuffle.astype(jnp.int32) + jnp.where(alive, 0, slot_total)
    picked = jnp.argsort(sort_key, axis=1).astype(jnp.int32)
    picked_dest = picked // pair_cap
    picked_turn = picked % pair_cap
    picked_alive = jnp.take_along_axis(alive, picked, axis=1)
    base = jnp.cumsum(counts, axis=0) - counts
    source = jnp.arange(device_total, dtype=jnp.int32)[:, None]
    rank_of = base[source, picked_dest] + picked_turn
    row_perm = jax.vmap(partial(jax.random.permutation, x=AUD_DEV))(jax.random.split(keys[4], device_total))
    row_of = row_perm[picked_dest, jnp.minimum(rank_of, AUD_DEV - 1)]
    dest_out = jnp.where(picked_alive, picked_dest, 0).reshape(-1).astype(jnp.int32)
    row_out = jnp.where(picked_alive, row_of, 0).reshape(-1).astype(jnp.int32)
    return (dest_out, row_out, jnp.sum(counts, axis=1).astype(jnp.int32))


def draw_dest_device(key, part):
    return route_tables(jax.random.fold_in(key, 7))[0]


def draw_dest_row(key, part):
    return route_tables(jax.random.fold_in(key, 7))[1]


def draw_live_count(key, part):
    return route_tables(jax.random.fold_in(key, 7))[2]


def with_spikes(drawn, key, source, target, parts, factor):
    owner, partner = [(jnp.arange(drawn.shape[dim]) // (drawn.shape[dim] // parts)).reshape([-1 if axis == dim else 1 for axis in range(drawn.ndim)]) for dim in (source, target)]
    chosen = jax.random.permutation(key, parts)[partner]
    strong = (owner == chosen) | (owner == (partner + parts // 2) % parts)
    return jnp.where(strong, factor * drawn, drawn)


def block_scale(own_key, shape, cuts, least, largest):
    def one(axis_at, parts):
        heights = jax.random.uniform(jax.random.fold_in(jax.random.fold_in(own_key, 6), axis_at), (parts,), jnp.float32, least / len(cuts), largest / len(cuts))
        return jnp.repeat(jnp.exp(heights), shape[axis_at] // parts).reshape((-1,) + (1,) * (len(shape) - axis_at - 1))

    factor_of = one(*cuts[0])
    for cut in cuts[1:]:
        factor_of = factor_of * one(*cut)
    return factor_of


def noise(rng, shape, width, limit, shards=(), held_as=jnp.bfloat16):
    drawn = jax.random.normal(rng, shape, jnp.float32) * width
    if len(shards) > 0:
        drawn = block_scale(rng, shape, shards, -0.22, 0.18) * drawn
    return jnp.clip(drawn, min=-limit, max=limit).astype(held_as)


def heavy_noise(own_key, shape, width, most, cuts, heavy, kind=jnp.bfloat16):
    entries = width * jax.random.normal(own_key, shape, jnp.float32)
    if cuts:
        entries = entries * block_scale(own_key, shape, cuts, -0.22, 0.18)
    return jnp.clip(with_spikes(entries, jax.random.fold_in(own_key, 3), *heavy), -most, most).astype(kind)


def setup_inputs(seed: int = 0) -> dict:
    key_of = jax.random.split(jax.random.key(seed), 10)
    queries = draw_queries(jax.random.fold_in(key_of[9], 71), 0)
    video_keys = draw_video_keys(jax.random.fold_in(key_of[9], 71), 0)
    video_values = noise(key_of[2], (RECS, VIDEO, D), 1.0, 6.0, ((0, 8), (1, 4)))
    out_weight = noise(key_of[3], (D, D), D ** -0.5, 0.15625)
    gate_logit = jnp.clip(jax.random.uniform(key_of[4], (1,), jnp.float32, 0.3, 1.2), 0.3, 1.2)
    row_grads = heavy_noise(key_of[5], (LLM_ROWS, D), 1.0, 6.0, ((0, 32),), (0, 1, 32, 2.75))
    dest_device = draw_dest_device(jax.random.fold_in(key_of[9], 71), 0)
    dest_row = draw_dest_row(jax.random.fold_in(key_of[9], 71), 0)
    live_count = draw_live_count(jax.random.fold_in(key_of[9], 71), 0)
    return dict(queries=queries, video_keys=video_keys, video_values=video_values, out_weight=out_weight, gate_logit=gate_logit, row_grads=row_grads, dest_device=dest_device, dest_row=dest_row, live_count=live_count)


def lowered(values):
    return lax.optimization_barrier(values.astype(jnp.bfloat16))


def head_blocks(query_rows, keys_all, values_all, grad_attn):
    inv_root = HEAD_DIM ** -0.5
    attn_parts = []
    query_parts = []
    key_parts = []
    value_parts = []
    for head_idx in range(HEADS):
        first_col = head_idx * HEAD_DIM
        query_heads = query_rows[:, first_col:first_col + HEAD_DIM].astype(jnp.float32)
        key_heads = keys_all[:, first_col:first_col + HEAD_DIM].astype(jnp.float32)
        value_heads = values_all[:, first_col:first_col + HEAD_DIM].astype(jnp.float32)
        grad_heads = grad_attn[:, first_col:first_col + HEAD_DIM].astype(jnp.float32)
        scores = jnp.dot(query_heads, key_heads.T) * inv_root
        row_peak = jnp.max(scores, axis=-1, keepdims=True)
        shifted = jnp.exp(scores - row_peak)
        softmax_w = shifted / jnp.sum(shifted, axis=-1, keepdims=True)
        probs_low = lowered(softmax_w).astype(jnp.float32)
        attn_low = lowered(jnp.dot(probs_low, value_heads))
        attn_wide = attn_low.astype(jnp.float32)
        row_delta = jnp.sum(grad_heads * attn_wide, axis=-1, keepdims=True)
        dprob = jnp.dot(grad_heads, value_heads.T)
        dscore = lowered(softmax_w * (dprob - row_delta)).astype(jnp.float32)
        query_parts.append(jnp.dot(dscore, key_heads) * inv_root)
        key_parts.append(jnp.dot(dscore.T, query_heads) * inv_root)
        value_parts.append(jnp.dot(probs_low.T, grad_heads))
        attn_parts.append(attn_low)
    return (jnp.concatenate(attn_parts, axis=1), jnp.concatenate(query_parts, axis=1),
            jnp.concatenate(key_parts, axis=1), jnp.concatenate(value_parts, axis=1))


def reference(queries, video_keys, video_values, out_weight, gate_logit, row_grads, dest_device, dest_row, live_count):
    slot_ids = jnp.arange(LLM_ROWS, dtype=jnp.int32)
    is_live = (slot_ids % LLM_DEV) < live_count[slot_ids // LLM_DEV]
    rec_index = jnp.where(is_live, dest_device % N_REC, RECS).astype(jnp.int32)
    audio_index = ((dest_device // N_REC) * AUD_DEV + dest_row).astype(jnp.int32)
    grad_y = jnp.zeros((RECS, AUDIO, D), jnp.bfloat16).at[rec_index, audio_index].set(row_grads, mode="drop")
    gate_value = jnp.tanh(gate_logit[0])
    weight_tr = out_weight.T

    def recording(carry, inputs):
        query_rec, key_rec, value_rec, grad_rec = inputs

        def block(inner, block_idx):
            key_acc, value_acc, weight_acc, gate_acc = inner
            block_start = (block_idx * AUD_DEV).astype(jnp.int32)
            query_blk = lax.dynamic_slice_in_dim(query_rec, block_start, AUD_DEV, 0)
            grad_blk = lax.dynamic_slice_in_dim(grad_rec, block_start, AUD_DEV, 0)
            upstream = jnp.dot(grad_blk, weight_tr, preferred_element_type=jnp.float32)
            grad_attn = (gate_value * upstream).astype(jnp.bfloat16)
            attn_low, query_grad, key_term, value_term = head_blocks(query_blk, key_rec, value_rec, grad_attn)
            key_acc = key_acc + lowered(key_term).astype(jnp.float32)
            value_acc = value_acc + lowered(value_term).astype(jnp.float32)
            weight_acc = weight_acc + gate_value * jnp.dot(grad_blk.T, attn_low, preferred_element_type=jnp.float32)
            gate_acc = gate_acc + jnp.sum(upstream * attn_low.astype(jnp.float32))
            return (key_acc, value_acc, weight_acc, gate_acc), query_grad.astype(jnp.bfloat16)

        zero_rows = jnp.zeros((VIDEO, D), jnp.float32)
        result, query_blocks = lax.scan(block, (zero_rows, zero_rows, carry[0], carry[1]), jnp.arange(N_CTX, dtype=jnp.int32))
        key_acc, value_acc, weight_acc, gate_acc = result
        return (weight_acc, gate_acc), (query_blocks.reshape(AUDIO, D), key_acc.astype(jnp.bfloat16), value_acc.astype(jnp.bfloat16))

    start_carry = (jnp.zeros((D, D), jnp.float32), jnp.zeros((), jnp.float32))
    totals, stacked = lax.scan(recording, start_carry, (queries, video_keys, video_values, grad_y))
    weight_acc, gate_acc = totals
    query_all, key_grads, value_grads = stacked
    picked = query_all[jnp.minimum(rec_index, RECS - 1), audio_index]
    query_grads = jnp.where(is_live[:, None], picked, jnp.zeros((), jnp.bfloat16))
    gate_grad = ((1.0 - gate_value * gate_value) * gate_acc).reshape(1)
    return query_grads, key_grads, value_grads, weight_acc, gate_grad
```

```python
import jax
import jax.numpy as jnp
from jax import lax
from jax.experimental import pallas as pl
from jax.experimental.pallas import tpu as pltpu
from jax.sharding import PartitionSpec as P

HEAD_DIM = 64
LANES = 128
VMEM_LIMIT = 48 * 1024 * 1024
NT = (((1,), (1,)), ((), ()))
NN = (((1,), (0,)), ((), ()))


def mm(left, right, dims=NN):
    return lax.dot_general(left, right, dims, preferred_element_type=jnp.float32)


def iota(shape, dim):
    return lax.broadcasted_iota(jnp.int32, shape, dim)


def params():
    return pltpu.CompilerParams(vmem_limit_bytes=VMEM_LIMIT)


def as_column(row_vector):
    wide = jnp.broadcast_to(row_vector, (LANES, row_vector.shape[1]))
    return jnp.transpose(wide)[:, :1]


def as_row(column_block):
    return jnp.transpose(column_block.astype(jnp.float32))[:1, :]


def prep_kernel(pair_cap, owners, live_ref, dest_ref, row_ref, grads_ref, send_ref, target_ref):
    slots, width = grads_ref.shape
    slot = iota((1, slots), 1)
    is_live = slot < live_ref[0]
    dest = dest_ref[...]
    hot = jnp.logical_and(iota((owners, slots), 0) == dest, is_live)
    hot_f = jnp.where(hot, 1.0, 0.0)
    earlier = jnp.where(iota((slots, slots), 0) < iota((slots, slots), 1), 1.0, 0.0)
    before = mm(hot_f.astype(jnp.bfloat16), earlier.astype(jnp.bfloat16))
    rank = jnp.sum(hot_f * before, axis=0, keepdims=True).astype(jnp.int32)
    target = jnp.where(is_live, dest * pair_cap + rank, slots)
    target_ref[...] = target
    chosen = iota((slots, slots), 0) == target
    place = jnp.where(chosen, 1.0, 0.0).astype(jnp.bfloat16)
    send_ref[:, :width] = mm(place, grads_ref[...]).astype(jnp.bfloat16)
    row_no = (row_ref[...] + 1).astype(jnp.float32)
    index = jnp.sum(jnp.where(chosen, row_no, 0.0), axis=1, keepdims=True)
    send_ref[:, width:] = jnp.broadcast_to(index, (slots, LANES)).astype(jnp.bfloat16)


def route_prep(live_count, dest_device, dest_row, row_grads, owners):
    slots, width = row_grads.shape
    kernel = lambda *refs: prep_kernel(slots // owners, owners, *refs)
    vmem = pl.BlockSpec(memory_space=pltpu.VMEM)
    return pl.pallas_call(
        kernel,
        out_shape=(
            jax.ShapeDtypeStruct((slots, width + LANES), jnp.bfloat16),
            jax.ShapeDtypeStruct((1, slots), jnp.int32),
        ),
        in_specs=[pl.BlockSpec(memory_space=pltpu.SMEM), vmem, vmem, vmem],
        out_specs=(vmem, vmem),
        compiler_params=params(),
        name="route_prep",
        cost_estimate=pl.CostEstimate(
            flops=2 * slots * slots * width,
            bytes_accessed=4 * slots * width,
            transcendentals=0,
        ),
    )(live_count, dest_device.reshape(1, slots), dest_row.reshape(1, slots), row_grads)


def head_masks(shape, dim):
    first = iota(shape, dim) < HEAD_DIM
    return first, jnp.logical_not(first)


def keep(mask, value):
    return jnp.where(mask, value, jnp.zeros((), value.dtype))


def forward_kernel(query_ref, key_ref, value_ref, attn_ref, stat_ref):
    rows = query_ref.shape[0]
    query = query_ref[...] * jnp.asarray(HEAD_DIM ** -0.5, jnp.bfloat16)
    keys = key_ref[...]
    values_tr = jnp.transpose(value_ref[...])
    for head, mask in enumerate(head_masks((rows, LANES), 1)):
        scores = mm(keys, keep(mask, query), NT)
        peak = jnp.max(scores, axis=0, keepdims=True)
        shifted = jnp.exp(scores - peak)
        inverse = 1.0 / jnp.sum(shifted, axis=0, keepdims=True)
        probs_low = (shifted * inverse).astype(jnp.bfloat16)
        span = slice(head * HEAD_DIM, (head + 1) * HEAD_DIM)
        attn_ref[span, :] = mm(values_tr[span, :], probs_low).astype(jnp.bfloat16)
        stat_ref[0, head : head + 1, :] = peak
        stat_ref[0, head + 2 : head + 3, :] = inverse


def attention_forward(queries, keys, values):
    rows, width = queries.shape
    tokens = keys.shape[0]
    pairs = width // LANES
    columns = lambda i: (0, i)
    return pl.pallas_call(
        forward_kernel,
        grid=(pairs,),
        out_shape=(
            jax.ShapeDtypeStruct((width, rows), jnp.bfloat16),
            jax.ShapeDtypeStruct((pairs, 8, rows), jnp.float32),
        ),
        in_specs=[
            pl.BlockSpec((rows, LANES), columns),
            pl.BlockSpec((tokens, LANES), columns),
            pl.BlockSpec((tokens, LANES), columns),
        ],
        out_specs=(
            pl.BlockSpec((LANES, rows), lambda i: (i, 0)),
            pl.BlockSpec((1, 8, rows), lambda i: (i, 0, 0)),
        ),
        compiler_params=params(),
        name="attention_forward",
        cost_estimate=pl.CostEstimate(
            flops=16 * rows * tokens * width,
            bytes_accessed=4 * tokens * width + 4 * rows * width,
            transcendentals=rows * tokens * width // HEAD_DIM,
        ),
    )(queries, keys, values)


def grads_kernel(
    gate_ref, recv_ref, weight_ref, attn_blk_ref, attn_ref,
    grad_t_ref, grad_ref, gate_out_ref, weight_out_ref, rows_ref, rows_t_ref,
):
    step = pl.program_id(0)
    slots = recv_ref.shape[0]
    rows, width = rows_ref.shape

    @pl.when(step == 0)
    def _():
        index = as_row(recv_ref[:, width:])
        place = index == (iota((rows, slots), 0) + 1).astype(jnp.float32)
        place = jnp.where(place, 1.0, 0.0).astype(jnp.bfloat16)
        owned = mm(place, recv_ref[:, :width]).astype(jnp.bfloat16)
        rows_ref[...] = owned
        rows_t_ref[...] = jnp.transpose(owned)
        gate_out_ref[...] = jnp.zeros_like(gate_out_ref)

    gate = jnp.tanh(jnp.full((1, LANES), gate_ref[0], jnp.float32))[:, :1]
    upstream = mm(weight_ref[...], rows_ref[...], NT)
    grad_t = (gate * upstream).astype(jnp.bfloat16)
    grad_t_ref[...] = grad_t
    grad_ref[...] = jnp.transpose(grad_t)
    product = upstream * attn_blk_ref[...].astype(jnp.float32)
    gate_out_ref[...] += jnp.sum(product, axis=0, keepdims=True)
    first = pl.multiple_of(step * LANES, LANES)
    block = mm(rows_t_ref[pl.ds(first, LANES), :], attn_ref[...], NT)
    weight_out_ref[...] = (gate * block).astype(jnp.bfloat16)


def output_grads(gate_logit, recv, out_weight, attn_t):
    slots = recv.shape[0]
    width, rows = attn_t.shape
    blocks = width // LANES
    whole = lambda i: (0, 0)
    down = lambda i: (i, 0)
    return pl.pallas_call(
        grads_kernel,
        grid=(blocks,),
        out_shape=(
            jax.ShapeDtypeStruct((width, rows), jnp.bfloat16),
            jax.ShapeDtypeStruct((rows, width), jnp.bfloat16),
            jax.ShapeDtypeStruct((1, rows), jnp.float32),
            jax.ShapeDtypeStruct((width, width), jnp.bfloat16),
        ),
        in_specs=[
            pl.BlockSpec(memory_space=pltpu.SMEM),
            pl.BlockSpec((slots, width + LANES), whole),
            pl.BlockSpec((LANES, width), down),
            pl.BlockSpec((LANES, rows), down),
            pl.BlockSpec((width, rows), whole),
        ],
        out_specs=(
            pl.BlockSpec((LANES, rows), down),
            pl.BlockSpec((rows, LANES), lambda i: (0, i)),
            pl.BlockSpec((1, rows), whole),
            pl.BlockSpec((LANES, width), down),
        ),
        scratch_shapes=[
            pltpu.VMEM((rows, width), jnp.bfloat16),
            pltpu.VMEM((width, rows), jnp.bfloat16),
        ],
        compiler_params=params(),
        name="output_grads",
        cost_estimate=pl.CostEstimate(
            flops=4 * rows * width * width + 2 * slots * rows * width,
            bytes_accessed=4 * width * width + 8 * rows * width,
            transcendentals=0,
        ),
    )(gate_logit, recv, out_weight, attn_t, attn_t)


def backward_kernel(
    query_ref, key_ref, value_ref, grad_ref, grad_t_ref, attn_ref, stat_ref, index_ref,
    key_out_ref, value_out_ref, back_ref,
):
    rows = query_ref.shape[0]
    slots = index_ref.shape[0]
    root = jnp.asarray(HEAD_DIM ** -0.5, jnp.bfloat16)
    query = query_ref[...] * root
    keys = key_ref[...]
    values = value_ref[...]
    keys_tr = jnp.transpose(keys)
    grad = grad_ref[...]
    grad_t = grad_t_ref[...]
    lane_masks = head_masks((rows, LANES), 1)
    row_masks = head_masks((LANES, rows), 0)
    key_term = None
    value_term = None
    query_parts = []
    for head in range(2):
        span = slice(head * HEAD_DIM, (head + 1) * HEAD_DIM)
        query_h = keep(lane_masks[head], query)
        grad_h = keep(lane_masks[head], grad)
        scores = mm(keys, query_h, NT)
        peak = stat_ref[0, head : head + 1, :]
        inverse = stat_ref[0, head + 2 : head + 3, :]
        probs = jnp.exp(scores - peak) * inverse
        probs_low = probs.astype(jnp.bfloat16)
        delta = jnp.sum(
            grad_t_ref[span, :].astype(jnp.float32) * attn_ref[span, :].astype(jnp.float32),
            axis=0,
            keepdims=True,
        )
        dprob = mm(values, keep(row_masks[head], grad_t))
        dscore = (probs * (dprob - delta)).astype(jnp.bfloat16)
        value_part = mm(probs_low, grad_h)
        key_part = mm(dscore, query_h)
        value_term = value_part if head == 0 else value_term + value_part
        key_term = key_part if head == 0 else key_term + key_part
        query_parts.append(mm(keys_tr[span, :], dscore) * (HEAD_DIM ** -0.5))
    key_out_ref[...] = key_term.astype(jnp.bfloat16)
    value_out_ref[...] = value_term.astype(jnp.bfloat16)
    query_grad = jnp.transpose(jnp.concatenate(query_parts, axis=0).astype(jnp.bfloat16))
    index = index_ref[...][:, :1].astype(jnp.float32)
    place = index == (iota((slots, rows), 1) + 1).astype(jnp.float32)
    place = jnp.where(place, 1.0, 0.0).astype(jnp.bfloat16)
    back_ref[...] = mm(place, query_grad).astype(jnp.bfloat16)


def attention_backward(queries, keys, values, grad, grad_t, attn_t, stats, recv):
    rows, width = queries.shape
    tokens = keys.shape[0]
    slots = recv.shape[0]
    pairs = width // LANES
    columns = lambda i: (0, i)
    down = lambda i: (i, 0)
    return pl.pallas_call(
        backward_kernel,
        grid=(pairs,),
        out_shape=(
            jax.ShapeDtypeStruct((tokens, width), jnp.bfloat16),
            jax.ShapeDtypeStruct((tokens, width), jnp.bfloat16),
            jax.ShapeDtypeStruct((slots, width), jnp.bfloat16),
        ),
        in_specs=[
            pl.BlockSpec((rows, LANES), columns),
            pl.BlockSpec((tokens, LANES), columns),
            pl.BlockSpec((tokens, LANES), columns),
            pl.BlockSpec((rows, LANES), columns),
            pl.BlockSpec((LANES, rows), down),
            pl.BlockSpec((LANES, rows), down),
            pl.BlockSpec((1, 8, rows), lambda i: (i, 0, 0)),
            pl.BlockSpec((slots, LANES), lambda i: (0, width // LANES)),
        ],
        out_specs=(
            pl.BlockSpec((tokens, LANES), columns),
            pl.BlockSpec((tokens, LANES), columns),
            pl.BlockSpec((slots, LANES), columns),
        ),
        compiler_params=params(),
        name="attention_backward",
        cost_estimate=pl.CostEstimate(
            flops=40 * rows * tokens * width,
            bytes_accessed=8 * tokens * width + 12 * rows * width,
            transcendentals=rows * tokens * width // HEAD_DIM,
        ),
    )(queries, keys, values, grad, grad_t, attn_t, stats, recv)


def pick_kernel(target_ref, returned_ref, out_ref):
    slots = out_ref.shape[0]
    target = as_column(target_ref[...].astype(jnp.float32))
    place = target == iota((slots, slots), 1).astype(jnp.float32)
    place = jnp.where(place, 1.0, 0.0).astype(jnp.bfloat16)
    out_ref[...] = mm(place, returned_ref[...]).astype(jnp.bfloat16)


def pick_rows(target, returned):
    slots, width = returned.shape
    vmem = pl.BlockSpec(memory_space=pltpu.VMEM)
    return pl.pallas_call(
        pick_kernel,
        out_shape=jax.ShapeDtypeStruct((slots, width), jnp.bfloat16),
        in_specs=[vmem, vmem],
        out_specs=vmem,
        compiler_params=params(),
        name="pick_rows",
        cost_estimate=pl.CostEstimate(
            flops=2 * slots * slots * width,
            bytes_accessed=4 * slots * width,
            transcendentals=0,
        ),
    )(target, returned)


def shift(value, step):
    count = lax.axis_size("ctx")
    pairs = [(i, (i + step) % count) for i in range(count)]
    return lax.ppermute(value, "ctx", pairs)


def gather_ring(chunk):
    count = lax.axis_size("ctx")
    parts = [chunk]
    ahead = behind = chunk
    half = chunk.shape[0] // 2
    for step in range(1, count // 2 + 1):
        if 2 * step == count:
            if count == 2:
                parts.append(shift(chunk, 1))
            else:
                parts.append(shift(ahead[:half], 1))
                parts.append(shift(behind[half:], -1))
        else:
            ahead = shift(ahead, 1)
            behind = shift(behind, -1)
            parts.append(ahead)
            parts.append(behind)
    return jnp.concatenate(parts, axis=0)


def add(left, right):
    return (left.astype(jnp.float32) + right.astype(jnp.float32)).astype(jnp.bfloat16)


def scatter_ring(terms):
    count = lax.axis_size("ctx")
    rows = terms.shape[0] // count
    half = rows // 2
    take = lambda part: terms[part * rows : (part + 1) * rows]
    from_ahead = from_behind = None
    for step in range(count // 2, 0, -1):
        if 2 * step == count:
            last = take(count - 1)
            from_ahead = shift(last[:half], -1)
            from_behind = shift(last[half:], 1)
            continue
        back = take(2 * step - 1)
        forth = take(2 * step)
        if 2 * step == count - 2:
            back = jnp.concatenate([add(back[:half], from_ahead), back[half:]], axis=0)
            forth = jnp.concatenate([forth[:half], add(forth[half:], from_behind)], axis=0)
        else:
            back = add(back, from_ahead)
            forth = add(forth, from_behind)
        from_ahead = shift(back, -1)
        from_behind = shift(forth, 1)
    own = take(0).astype(jnp.float32)
    total = own + from_ahead.astype(jnp.float32) + from_behind.astype(jnp.float32)
    return total.astype(jnp.bfloat16)


def scatter_weight(term):
    ctx_count = lax.axis_size("ctx")
    rec_count = lax.axis_size("rec")
    width = term.shape[1]
    rows = term.shape[0] // (ctx_count * rec_count)
    rec = lax.axis_index("rec")
    left = rec_count
    bit = 0
    while left > 1:
        left //= 2
        term = term.reshape(ctx_count, left, 2, rows, width)
        mine = (rec >> bit) & 1
        sent = lax.dynamic_index_in_dim(term, 1 - mine, 2, keepdims=False)
        kept = lax.dynamic_index_in_dim(term, mine, 2, keepdims=False)
        got = lax.ppermute(sent, "rec", [(i, i ^ (1 << bit)) for i in range(rec_count)])
        term = add(kept, got)
        bit += 1
    term = term.reshape(ctx_count, rows, width)
    parts = lax.all_to_all(term, "ctx", split_axis=0, concat_axis=0, tiled=True)
    return jnp.sum(parts.astype(jnp.float32), axis=0)


def exchange(value, count):
    slots, width = value.shape
    moved = lax.all_to_all(
        value.reshape(count, slots // count, width),
        ("ctx", "rec"),
        split_axis=0,
        concat_axis=0,
        tiled=True,
    )
    return moved.reshape(slots, width)


def local(
    queries,
    video_keys,
    video_values,
    out_weight,
    gate_logit,
    row_grads,
    dest_device,
    dest_row,
    live_count,
):
    count = lax.axis_size("ctx") * lax.axis_size("rec")
    keys = gather_ring(video_keys[0])
    values = gather_ring(video_values[0])
    send, target = route_prep(live_count, dest_device, dest_row, row_grads, count)
    recv = exchange(send, count)
    attn_t, stats = attention_forward(queries[0], keys, values)
    grad_t, grad, gate_part, weight_term = output_grads(gate_logit, recv, out_weight, attn_t)
    weight_grad = scatter_weight(weight_term)
    key_term, value_term, back = attention_backward(
        queries[0], keys, values, grad, grad_t, attn_t, stats, recv
    )
    key_sum = scatter_ring(key_term)
    value_sum = scatter_ring(value_term)
    gate_row = jnp.broadcast_to(jnp.sum(gate_part), (count, 1, LANES))
    gate_parts = lax.all_to_all(
        gate_row, ("ctx", "rec"), split_axis=0, concat_axis=0, tiled=True
    )
    gate_total = jnp.sum(gate_parts[:, 0, 0])
    gate_value = jnp.tanh(gate_logit[0])
    gate_grad = (1.0 - gate_value * gate_value) * gate_total
    query_grads = pick_rows(target, exchange(back, count))
    return query_grads, key_sum[None], value_sum[None], weight_grad, gate_grad.reshape(1)


def solution(mesh):
    in_specs = (
        P("rec", "ctx", None),
        P("rec", "ctx", None),
        P("rec", "ctx", None),
        P(),
        P(),
        P(("ctx", "rec"), None),
        P(("ctx", "rec")),
        P(("ctx", "rec")),
        P(("ctx", "rec")),
    )
    out_specs = (
        P(("ctx", "rec"), None),
        P("rec", "ctx", None),
        P("rec", "ctx", None),
        P(("ctx", "rec"), None),
        P(),
    )
    return jax.shard_map(local, mesh=mesh, in_specs=in_specs, out_specs=out_specs, check_vma=False)
```

```python
import jax
import jax.numpy as jnp
from jax import lax
from jax.experimental import pallas as pl
from jax.experimental.pallas import tpu as pltpu
from jax.sharding import PartitionSpec as P

HEAD_DIM = 64
LANES = 128
VMEM_LIMIT = 32 * 1024 * 1024
VMEM_WHOLE = 62 * 1024 * 1024
ATTENTION_COST = 150
FAR_COST = 300000
STEP_COST = 74000
NT = (((1,), (1,)), ((), ()))
NN = (((1,), (0,)), ((), ()))


def mm(left, right, dims=NN):
    return lax.dot_general(left, right, dims, preferred_element_type=jnp.float32)


def iota(shape, dim):
    return lax.broadcasted_iota(jnp.int32, shape, dim)


def params(limit=VMEM_LIMIT):
    return pltpu.CompilerParams(vmem_limit_bytes=limit)


def as_column(row_vector):
    wide = jnp.broadcast_to(row_vector, (LANES, row_vector.shape[1]))
    return jnp.transpose(wide)[:, :1]


def as_row(column_block):
    return jnp.transpose(column_block.astype(jnp.float32))[:1, :]


def prep_kernel(pair_cap, owners, live_ref, dest_ref, row_ref, grads_ref, send_ref, target_ref):
    slots, width = grads_ref.shape
    slot = iota((1, slots), 1)
    is_live = slot < live_ref[0]
    dest = dest_ref[...]
    hot = jnp.logical_and(iota((owners, slots), 0) == dest, is_live)
    hot_f = jnp.where(hot, 1.0, 0.0)
    earlier = jnp.where(iota((slots, slots), 0) < iota((slots, slots), 1), 1.0, 0.0)
    before = mm(hot_f.astype(jnp.bfloat16), earlier.astype(jnp.bfloat16))
    rank = jnp.sum(hot_f * before, axis=0, keepdims=True).astype(jnp.int32)
    target = jnp.where(is_live, dest * pair_cap + rank, slots)
    target_ref[...] = target
    chosen = iota((slots, slots), 0) == target
    place = jnp.where(chosen, 1.0, 0.0).astype(jnp.bfloat16)
    send_ref[:, :width] = mm(place, grads_ref[...]).astype(jnp.bfloat16)
    row_no = (row_ref[...] + 1).astype(jnp.float32)
    index = jnp.sum(jnp.where(chosen, row_no, 0.0), axis=1, keepdims=True)
    send_ref[:, width:] = jnp.broadcast_to(index, (slots, LANES)).astype(jnp.bfloat16)


def route_prep(live_count, dest_device, dest_row, row_grads, owners):
    slots, width = row_grads.shape
    kernel = lambda *refs: prep_kernel(slots // owners, owners, *refs)
    vmem = pl.BlockSpec(memory_space=pltpu.VMEM)
    return pl.pallas_call(
        kernel,
        out_shape=(
            jax.ShapeDtypeStruct((slots, width + LANES), jnp.bfloat16),
            jax.ShapeDtypeStruct((1, slots), jnp.int32),
        ),
        in_specs=[pl.BlockSpec(memory_space=pltpu.SMEM), vmem, vmem, vmem],
        out_specs=(vmem, vmem),
        compiler_params=params(),
        name="route_prep",
        cost_estimate=pl.CostEstimate(
            flops=2 * slots * slots * width,
            bytes_accessed=4 * slots * width,
            transcendentals=0,
        ),
    )(live_count, dest_device.reshape(1, slots), dest_row.reshape(1, slots), row_grads)


def head_masks(shape, dim):
    first = iota(shape, dim) < HEAD_DIM
    return first, jnp.logical_not(first)


def keep(mask, value):
    return jnp.where(mask, value, jnp.zeros((), value.dtype))


def unpack_kernel(recv_ref, rows_ref, rows_t_ref):
    slots = recv_ref.shape[0]
    rows, width = rows_ref.shape
    index = as_row(recv_ref[:, width:])
    place = index == (iota((rows, slots), 0) + 1).astype(jnp.float32)
    place = jnp.where(place, 1.0, 0.0).astype(jnp.bfloat16)
    owned = mm(place, recv_ref[:, :width]).astype(jnp.bfloat16)
    rows_ref[...] = owned
    rows_t_ref[...] = jnp.transpose(owned)


def unpack_rows(recv, rows):
    slots, width = recv.shape
    width -= LANES
    vmem = pl.BlockSpec(memory_space=pltpu.VMEM)
    return pl.pallas_call(
        unpack_kernel,
        out_shape=(
            jax.ShapeDtypeStruct((rows, width), jnp.bfloat16),
            jax.ShapeDtypeStruct((width, rows), jnp.bfloat16),
        ),
        in_specs=[vmem],
        out_specs=(vmem, vmem),
        compiler_params=params(),
        name="unpack_rows",
        cost_estimate=pl.CostEstimate(
            flops=2 * slots * rows * width,
            bytes_accessed=2 * (slots + 2 * rows) * width,
            transcendentals=0,
        ),
    )(recv)


def attend(gate_ref, query_ref, weight_ref, rows_ref, index_ref, keys, values,
           attn_ref, back_ref, gate_out_ref):
    rows = query_ref.shape[0]
    slots = index_ref.shape[0]
    root = HEAD_DIM ** -0.5
    query = query_ref[...] * jnp.asarray(root, jnp.bfloat16)
    keys_tr = jnp.transpose(keys)
    values_tr = jnp.transpose(values)
    gate = jnp.tanh(jnp.full((1, LANES), gate_ref[0], jnp.float32))[:, :1]
    upstream = mm(weight_ref[...], rows_ref[...], NT)
    grad_t = (gate * upstream).astype(jnp.bfloat16)
    grad = jnp.transpose(grad_t)
    lane_masks = head_masks((rows, LANES), 1)
    row_masks = head_masks((LANES, rows), 0)
    key_term = None
    value_term = None
    query_parts = []
    gate_sum = None
    for head in range(2):
        span = slice(head * HEAD_DIM, (head + 1) * HEAD_DIM)
        query_h = keep(lane_masks[head], query)
        grad_h = keep(lane_masks[head], grad)
        scores = mm(keys, query_h, NT)
        peak = jnp.max(scores, axis=0, keepdims=True)
        shifted = jnp.exp(scores - peak)
        inverse = 1.0 / jnp.sum(shifted, axis=0, keepdims=True)
        probs = shifted * inverse
        probs_low = probs.astype(jnp.bfloat16)
        attn_h = mm(values_tr[span, :], probs_low).astype(jnp.bfloat16)
        attn_ref[span, :] = attn_h
        attn_wide = attn_h.astype(jnp.float32)
        delta = jnp.sum(grad_t[span, :].astype(jnp.float32) * attn_wide, axis=0, keepdims=True)
        gate_h = jnp.sum(upstream[span, :] * attn_wide, axis=0, keepdims=True)
        dprob = mm(values, keep(row_masks[head], grad_t))
        dscore = (probs * (dprob - delta)).astype(jnp.bfloat16)
        value_part = mm(probs_low, grad_h)
        key_part = mm(dscore, query_h)
        value_term = value_part if head == 0 else value_term + value_part
        key_term = key_part if head == 0 else key_term + key_part
        gate_sum = gate_h if head == 0 else gate_sum + gate_h
        query_parts.append(mm(keys_tr[span, :], dscore) * root)
    gate_out_ref[...] += gate_sum
    query_grad = jnp.transpose(jnp.concatenate(query_parts, axis=0).astype(jnp.bfloat16))
    index = index_ref[...][:, :1].astype(jnp.float32)
    place = index == (iota((slots, rows), 1) + 1).astype(jnp.float32)
    place = jnp.where(place, 1.0, 0.0).astype(jnp.bfloat16)
    back_ref[...] = mm(place, query_grad).astype(jnp.bfloat16)
    return key_term.astype(jnp.bfloat16), value_term.astype(jnp.bfloat16)


def gate_lanes(total, shape):
    high = total.astype(jnp.bfloat16).astype(jnp.float32)
    middle = (total - high).astype(jnp.bfloat16).astype(jnp.float32)
    low = total - high - middle
    lane = iota(shape, 1)
    terms = jnp.where(lane == 0, high, jnp.where(lane == 1, middle, low))
    return jnp.where(lane < 3, terms, 0.0).astype(jnp.bfloat16)


def attention_kernel(blocks, pairs, gate_ref, before_ref, query_ref, weight_ref, rows_ref,
                     index_ref, *refs):
    parts, outs = refs[: blocks + 1], refs[blocks + 1 : 2 * blocks + 2]
    attn_ref, back_ref, gate_out_ref = refs[2 * blocks + 2 :]
    step = pl.program_id(0)

    @pl.when(step == 0)
    def _():
        gate_out_ref[...] = before_ref[...]

    @pl.when(step < pairs)
    def _():
        chunk = parts[-1].shape[0]
        keys = jnp.concatenate([part[:chunk] for part in parts[:-1]], axis=0)
        values = jnp.concatenate(
            [part[chunk:] for part in parts[:-2]] + [parts[-1][...]], axis=0
        )
        key_term, value_term = attend(
            gate_ref, query_ref, weight_ref, rows_ref, index_ref, keys, values,
            attn_ref, back_ref, gate_out_ref,
        )
        for number, out in enumerate(outs[:-2]):
            span = slice(number * chunk, (number + 1) * chunk)
            out[:chunk] = key_term[span]
            out[chunk:] = value_term[span]
        outs[-2][...] = key_term[-chunk:]
        outs[-1][...] = value_term[-chunk:]

    @pl.when(step == pairs)
    def _():
        total = jnp.sum(gate_out_ref[...], axis=1, keepdims=True)
        back_ref[...] = gate_lanes(total, back_ref.shape)


def attention(gate_logit, before, queries, out_weight, grad_rows, recv, parts, first_pair, extra):
    rows, width = queries.shape
    slots = recv.shape[0]
    span = parts[0].shape[1]
    pairs = span // LANES
    tokens = (len(parts) - 1) * parts[-1].shape[0]
    at = lambda i: jnp.minimum(i, pairs - 1)
    columns = lambda i: (0, at(i))
    part_specs = [pl.BlockSpec((part.shape[0], LANES), columns) for part in parts]
    whole = lambda i: (0, 0)
    outs = pl.pallas_call(
        lambda *refs: attention_kernel(len(parts) - 1, pairs, *refs),
        grid=(pairs + extra,),
        out_shape=(
            *[jax.ShapeDtypeStruct(part.shape, jnp.bfloat16) for part in parts],
            jax.ShapeDtypeStruct((span, rows), jnp.bfloat16),
            jax.ShapeDtypeStruct((slots, span + extra * LANES), jnp.bfloat16),
            jax.ShapeDtypeStruct((1, rows), jnp.float32),
        ),
        in_specs=[
            pl.BlockSpec(memory_space=pltpu.SMEM),
            pl.BlockSpec((1, rows), whole),
            pl.BlockSpec((rows, LANES), lambda i: (0, at(i) + first_pair)),
            pl.BlockSpec((LANES, width), lambda i: (at(i) + first_pair, 0)),
            pl.BlockSpec((rows, width), whole),
            pl.BlockSpec((slots, LANES), lambda i: (0, width // LANES)),
            *part_specs,
        ],
        out_specs=(
            *part_specs,
            pl.BlockSpec((LANES, rows), lambda i: (at(i), 0)),
            pl.BlockSpec((slots, LANES), lambda i: (0, i)),
            pl.BlockSpec((1, rows), whole),
        ),
        compiler_params=params(VMEM_WHOLE),
        name="attention",
        cost_estimate=pl.CostEstimate(
            flops=ATTENTION_COST * rows * tokens * span,
            bytes_accessed=8 * tokens * span + 12 * rows * span,
            transcendentals=rows * tokens * span // HEAD_DIM,
        ),
    )(gate_logit, before, queries, out_weight, grad_rows, recv, *parts)
    return outs[: len(parts)], *outs[len(parts) :]


def weight_kernel(gate_ref, rows_t_ref, first_ref, second_ref, out_ref):
    gate = jnp.tanh(jnp.full((1, LANES), gate_ref[0], jnp.float32))[:, :1]
    half = first_ref.shape[0]
    for number, attn_ref in enumerate((first_ref, second_ref)):
        block = mm(rows_t_ref[...], attn_ref[...], NT)
        out_ref[:, number * half : (number + 1) * half] = (gate * block).astype(jnp.bfloat16)


def weight_term(gate_logit, rows_t, first_attn, second_attn):
    width, rows = rows_t.shape
    steps = 5
    return pl.pallas_call(
        weight_kernel,
        grid=(steps,),
        out_shape=jax.ShapeDtypeStruct((width, width), jnp.bfloat16),
        in_specs=[
            pl.BlockSpec(memory_space=pltpu.SMEM),
            pl.BlockSpec((width // steps, rows), lambda i: (i, 0)),
            pl.BlockSpec((width // 2, rows), lambda i: (0, 0)),
            pl.BlockSpec((width // 2, rows), lambda i: (0, 0)),
        ],
        out_specs=pl.BlockSpec((width // steps, width), lambda i: (i, 0)),
        compiler_params=params(),
        name="weight_term",
        cost_estimate=pl.CostEstimate(
            flops=2 * rows * width * width,
            bytes_accessed=2 * width * width + 4 * rows * width,
            transcendentals=0,
        ),
    )(gate_logit, rows_t, first_attn, second_attn)


def pick_kernel(pair_cap, target_ref, first_ref, second_ref, out_ref, gate_ref):
    slots, half = first_ref.shape
    target = as_column(target_ref[...].astype(jnp.float32))
    place = target == iota((slots, slots), 1).astype(jnp.float32)
    place = jnp.where(place, 1.0, 0.0).astype(jnp.bfloat16)
    out_ref[:, :half] = mm(place, first_ref[...]).astype(jnp.bfloat16)
    out_ref[:, half:] = mm(place, second_ref[:, :half]).astype(jnp.bfloat16)
    shares = second_ref[:, half:].astype(jnp.float32)
    shares = jnp.where(iota(shares.shape, 0) % pair_cap == 0, shares, 0.0)
    gate_ref[...] = jnp.sum(jnp.sum(shares, axis=0, keepdims=True), axis=1, keepdims=True)


def pick_rows(target, first, second, pair_cap):
    slots, half = first.shape
    vmem = pl.BlockSpec(memory_space=pltpu.VMEM)
    return pl.pallas_call(
        lambda *refs: pick_kernel(pair_cap, *refs),
        out_shape=(
            jax.ShapeDtypeStruct((slots, 2 * half), jnp.bfloat16),
            jax.ShapeDtypeStruct((1, 1), jnp.float32),
        ),
        in_specs=[vmem, vmem, vmem],
        out_specs=(vmem, vmem),
        compiler_params=params(),
        name="pick_rows",
        cost_estimate=pl.CostEstimate(
            flops=4 * slots * slots * half,
            bytes_accessed=8 * slots * half,
            transcendentals=0,
        ),
    )(target, first, second)


def shift(value, step):
    count = lax.axis_size("ctx")
    pairs = [(i, (i + step) % count) for i in range(count)]
    return lax.ppermute(value, "ctx", pairs)


def gather_near(chunk):
    parts = [chunk]
    ahead = behind = chunk
    for _ in range(1, lax.axis_size("ctx") // 2):
        ahead = shift(ahead, 1)
        behind = shift(behind, -1)
        parts += [ahead, behind]
    return parts


def halves_kernel(ahead_ref, behind_ref, keys_ref, values_ref):
    half = keys_ref.shape[0]
    keys_ref[...] = ahead_ref[:half]
    values_ref[...] = behind_ref[half:]


def farthest(ahead, behind, cost):
    half = ahead.shape[0] // 2
    vmem = pl.BlockSpec(memory_space=pltpu.VMEM)
    return pl.pallas_call(
        halves_kernel,
        out_shape=(jax.ShapeDtypeStruct((half, ahead.shape[1]), ahead.dtype),) * 2,
        in_specs=[vmem, vmem],
        out_specs=(vmem, vmem),
        compiler_params=params(),
        name="farthest",
        cost_estimate=pl.CostEstimate(
            flops=cost * ahead.size, bytes_accessed=4 * ahead.size, transcendentals=0
        ),
    )(ahead, behind)


def gather_far(parts, cost):
    keys, values = farthest(parts[-2], parts[-1], cost)
    return [*parts, shift(keys, 1), shift(values, -1)]


def add(left, right):
    return (left.astype(jnp.float32) + right.astype(jnp.float32)).astype(jnp.bfloat16)


def start_sums(parts):
    return shift(parts[-2], -1), shift(parts[-1], 1)


def step_kernel(back_ref, forth_ref, far_keys_ref, far_values_ref, back_out_ref, forth_out_ref):
    half = far_keys_ref.shape[0]
    back_out_ref[:half] = add(back_ref[:half], far_keys_ref[...])
    back_out_ref[half:] = back_ref[half:]
    forth_out_ref[:half] = forth_ref[:half]
    forth_out_ref[half:] = add(forth_ref[half:], far_values_ref[...])


def step_sums(back, forth, far_keys, far_values):
    vmem = pl.BlockSpec(memory_space=pltpu.VMEM)
    return pl.pallas_call(
        step_kernel,
        out_shape=(jax.ShapeDtypeStruct(back.shape, back.dtype),) * 2,
        in_specs=[vmem] * 4,
        out_specs=(vmem, vmem),
        compiler_params=params(),
        name="step_sums",
        cost_estimate=pl.CostEstimate(
            flops=STEP_COST * back.size,
            bytes_accessed=8 * back.size,
            transcendentals=0,
        ),
    )(back, forth, far_keys, far_values)


def finish_sums(parts, far_keys, far_values):
    half = far_keys.shape[0]
    steps = lax.axis_size("ctx") // 2 - 1
    back, forth = step_sums(parts[2 * steps - 1], parts[2 * steps], far_keys, far_values)
    for step in range(steps, 0, -1):
        if step < steps:
            back = add(parts[2 * step - 1], back)
            forth = add(parts[2 * step], forth)
        back = shift(back, -1)
        forth = shift(forth, 1)
    own = parts[0].astype(jnp.float32)
    total = own + back.astype(jnp.float32) + forth.astype(jnp.float32)
    total = total.astype(jnp.bfloat16)
    return total[:half], total[half:]


def halve(term, bit):
    rec_count = lax.axis_size("rec")
    ctx_count, left, rows, width = term.shape
    term = term.reshape(ctx_count, left // 2, 2, rows, width)
    mine = (lax.axis_index("rec") >> bit) & 1
    sent = lax.dynamic_index_in_dim(term, 1 - mine, 2, keepdims=False)
    kept = lax.dynamic_index_in_dim(term, mine, 2, keepdims=False)
    return add(kept, lax.ppermute(sent, "rec", [(i, i ^ (1 << bit)) for i in range(rec_count)]))


def sum_blocks(term):
    ctx_count = lax.axis_size("ctx")
    block = lax.axis_index("ctx")
    total = lax.dynamic_index_in_dim(term, block, 0, keepdims=False).astype(jnp.float32)
    for step in range(1, ctx_count):
        sent = lax.dynamic_index_in_dim(term, block ^ step, 0, keepdims=False)
        pairs = [(i, i ^ step) for i in range(ctx_count)]
        total = total + lax.ppermute(sent, "ctx", pairs).astype(jnp.float32)
    return total


def exchange(value, count):
    slots, width = value.shape
    moved = lax.all_to_all(
        value.reshape(count, slots // count, width),
        ("ctx", "rec"),
        split_axis=0,
        concat_axis=0,
        tiled=True,
    )
    return moved.reshape(slots, width)


def local(
    queries,
    video_keys,
    video_values,
    out_weight,
    gate_logit,
    row_grads,
    dest_device,
    dest_row,
    live_count,
):
    count = lax.axis_size("ctx") * lax.axis_size("rec")
    rows, width = queries.shape[1:]
    half = width // 2
    tie = lax.optimization_barrier
    first, second = (
        jnp.concatenate([video_keys[0][:, part], video_values[0][:, part]], axis=0)
        for part in (slice(0, half), slice(half, width))
    )
    first_parts = gather_far(gather_near(first), FAR_COST)
    send, target = route_prep(live_count, dest_device, dest_row, row_grads, count)
    recv = exchange(send, count)
    recv, second = tie((recv, second))
    second_parts = gather_near(second)
    grad_rows, rows_t = unpack_rows(recv, rows)
    common = (queries[0], out_weight, grad_rows, recv)
    first_terms, first_attn, first_back, gate_part = attention(
        gate_logit, jnp.zeros((1, rows), jnp.float32), *common, first_parts, 0, 0
    )
    first_far = start_sums(first_terms)
    first_returned = exchange(first_back, count)
    second_parts, gate_part = tie((second_parts, gate_part))
    second_parts = gather_far(second_parts, 1)
    second_terms, second_attn, second_back, _ = attention(
        gate_logit, gate_part, *common, second_parts, half // LANES, 1
    )
    second_far = start_sums(second_terms)
    first_far, second_attn = tie((first_far, second_attn))
    product = weight_term(gate_logit, rows_t, first_attn, second_attn)
    first_returned, product = tie((first_returned, product))
    blocks, devices = lax.axis_size("ctx"), lax.axis_size("rec")
    product = halve(product.reshape(blocks, devices, width // count, width), 0)
    second_returned = exchange(second_back, count)
    first_sum = finish_sums(first_terms, *first_far)
    bit = 1
    while product.shape[1] > 1:
        product = halve(product, bit)
        bit += 1
    second_far, weight_chips = tie((second_far, product[:, 0]))
    second_sum = finish_sums(second_terms, *second_far)
    weight_grad = sum_blocks(weight_chips)
    query_grads, gate_total = pick_rows(
        target, first_returned, second_returned, row_grads.shape[0] // count
    )
    gate_value = jnp.tanh(gate_logit[0])
    gate_grad = (1.0 - gate_value * gate_value) * gate_total[0, 0]
    key_sum, value_sum = (jnp.concatenate(pair, axis=1) for pair in zip(first_sum, second_sum))
    return query_grads, key_sum[None], value_sum[None], weight_grad, gate_grad.reshape(1)


def solution(mesh):
    in_specs = (
        P("rec", "ctx", None),
        P("rec", "ctx", None),
        P("rec", "ctx", None),
        P(),
        P(),
        P(("ctx", "rec"), None),
        P(("ctx", "rec")),
        P(("ctx", "rec")),
        P(("ctx", "rec")),
    )
    out_specs = (
        P(("ctx", "rec"), None),
        P("rec", "ctx", None),
        P("rec", "ctx", None),
        P(("ctx", "rec"), None),
        P(),
    )
    return jax.shard_map(local, mesh=mesh, in_specs=in_specs, out_specs=out_specs, check_vma=False)
```

```python
import jax
import jax.numpy as jnp
from jax import lax
from jax.experimental import pallas as pl
from jax.experimental.pallas import tpu as pltpu
from jax.sharding import PartitionSpec as P

HEAD_DIM = 64
LANES = 128
VMEM_LIMIT = 32 * 1024 * 1024
VMEM_WHOLE = 62 * 1024 * 1024
ATTENTION_COST = 150
FAR_COST = 300000
STEP_COST = 74000
TOTAL_COST = 150000
NT = (((1,), (1,)), ((), ()))
NN = (((1,), (0,)), ((), ()))


def mm(left, right, dims=NN):
    return lax.dot_general(left, right, dims, preferred_element_type=jnp.float32)


def iota(shape, dim):
    return lax.broadcasted_iota(jnp.int32, shape, dim)


def params(limit=VMEM_LIMIT):
    return pltpu.CompilerParams(vmem_limit_bytes=limit)


def as_column(row_vector):
    wide = jnp.broadcast_to(row_vector, (LANES, row_vector.shape[1]))
    return jnp.transpose(wide)[:, :1]


def as_row(column_block):
    return jnp.transpose(column_block.astype(jnp.float32))[:1, :]


def prep_kernel(pair_cap, owners, live_ref, dest_ref, row_ref, grads_ref, send_ref, target_ref):
    slots, width = grads_ref.shape
    slot = iota((1, slots), 1)
    is_live = slot < live_ref[0]
    dest = dest_ref[...]
    hot = jnp.logical_and(iota((owners, slots), 0) == dest, is_live)
    hot_f = jnp.where(hot, 1.0, 0.0)
    earlier = jnp.where(iota((slots, slots), 0) < iota((slots, slots), 1), 1.0, 0.0)
    before = mm(hot_f.astype(jnp.bfloat16), earlier.astype(jnp.bfloat16))
    rank = jnp.sum(hot_f * before, axis=0, keepdims=True).astype(jnp.int32)
    target = jnp.where(is_live, dest * pair_cap + rank, slots)
    target_ref[...] = target
    chosen = iota((slots, slots), 0) == target
    place = jnp.where(chosen, 1.0, 0.0).astype(jnp.bfloat16)
    send_ref[:, :width] = mm(place, grads_ref[...]).astype(jnp.bfloat16)
    row_no = (row_ref[...] + 1).astype(jnp.float32)
    index = jnp.sum(jnp.where(chosen, row_no, 0.0), axis=1, keepdims=True)
    send_ref[:, width:] = jnp.broadcast_to(index, (slots, LANES)).astype(jnp.bfloat16)


def route_prep(live_count, dest_device, dest_row, row_grads, owners):
    slots, width = row_grads.shape
    kernel = lambda *refs: prep_kernel(slots // owners, owners, *refs)
    vmem = pl.BlockSpec(memory_space=pltpu.VMEM)
    return pl.pallas_call(
        kernel,
        out_shape=(
            jax.ShapeDtypeStruct((slots, width + LANES), jnp.bfloat16),
            jax.ShapeDtypeStruct((1, slots), jnp.int32),
        ),
        in_specs=[pl.BlockSpec(memory_space=pltpu.SMEM), vmem, vmem, vmem],
        out_specs=(vmem, vmem),
        compiler_params=params(),
        name="route_prep",
        cost_estimate=pl.CostEstimate(
            flops=2 * slots * slots * width,
            bytes_accessed=4 * slots * width,
            transcendentals=0,
        ),
    )(live_count, dest_device.reshape(1, slots), dest_row.reshape(1, slots), row_grads)


def head_masks(shape, dim):
    first = iota(shape, dim) < HEAD_DIM
    return first, jnp.logical_not(first)


def keep(mask, value):
    return jnp.where(mask, value, jnp.zeros((), value.dtype))


def unpack_kernel(recv_ref, rows_ref, rows_t_ref):
    slots = recv_ref.shape[0]
    rows, width = rows_ref.shape
    index = as_row(recv_ref[:, width:])
    place = index == (iota((rows, slots), 0) + 1).astype(jnp.float32)
    place = jnp.where(place, 1.0, 0.0).astype(jnp.bfloat16)
    owned = mm(place, recv_ref[:, :width]).astype(jnp.bfloat16)
    rows_ref[...] = owned
    rows_t_ref[...] = jnp.transpose(owned)


def unpack_rows(recv, rows):
    slots, width = recv.shape
    width -= LANES
    vmem = pl.BlockSpec(memory_space=pltpu.VMEM)
    return pl.pallas_call(
        unpack_kernel,
        out_shape=(
            jax.ShapeDtypeStruct((rows, width), jnp.bfloat16),
            jax.ShapeDtypeStruct((width, rows), jnp.bfloat16),
        ),
        in_specs=[vmem],
        out_specs=(vmem, vmem),
        compiler_params=params(),
        name="unpack_rows",
        cost_estimate=pl.CostEstimate(
            flops=2 * slots * rows * width,
            bytes_accessed=2 * (slots + 2 * rows) * width,
            transcendentals=0,
        ),
    )(recv)


def attend(gate_ref, query_ref, weight_ref, rows_ref, rows_t_ref, index_ref, keys, values,
           product_ref, back_ref, gate_out_ref):
    rows = query_ref.shape[0]
    slots = index_ref.shape[0]
    root = HEAD_DIM ** -0.5
    query = query_ref[...] * jnp.asarray(root, jnp.bfloat16)
    keys_tr = jnp.transpose(keys)
    values_tr = jnp.transpose(values)
    gate = jnp.tanh(jnp.full((1, LANES), gate_ref[0], jnp.float32))[:, :1]
    upstream = mm(weight_ref[...], rows_ref[...], NT)
    grad_t = (gate * upstream).astype(jnp.bfloat16)
    grad = jnp.transpose(grad_t)
    lane_masks = head_masks((rows, LANES), 1)
    row_masks = head_masks((LANES, rows), 0)
    key_term = None
    value_term = None
    query_parts = []
    attn_parts = []
    gate_sum = None
    for head in range(2):
        span = slice(head * HEAD_DIM, (head + 1) * HEAD_DIM)
        query_h = keep(lane_masks[head], query)
        grad_h = keep(lane_masks[head], grad)
        scores = mm(keys, query_h, NT)
        peak = jnp.max(scores, axis=0, keepdims=True)
        shifted = jnp.exp(scores - peak)
        inverse = 1.0 / jnp.sum(shifted, axis=0, keepdims=True)
        probs = shifted * inverse
        probs_low = probs.astype(jnp.bfloat16)
        attn_h = mm(values_tr[span, :], probs_low).astype(jnp.bfloat16)
        attn_parts.append(attn_h)
        attn_wide = attn_h.astype(jnp.float32)
        delta = jnp.sum(grad_t[span, :].astype(jnp.float32) * attn_wide, axis=0, keepdims=True)
        gate_h = jnp.sum(upstream[span, :] * attn_wide, axis=0, keepdims=True)
        dprob = mm(values, keep(row_masks[head], grad_t))
        dscore = (probs * (dprob - delta)).astype(jnp.bfloat16)
        value_part = mm(probs_low, grad_h)
        key_part = mm(dscore, query_h)
        value_term = value_part if head == 0 else value_term + value_part
        key_term = key_part if head == 0 else key_term + key_part
        gate_sum = gate_h if head == 0 else gate_sum + gate_h
        query_parts.append(mm(keys_tr[span, :], dscore) * root)
    gate_out_ref[...] += gate_sum
    product = mm(rows_t_ref[...], jnp.concatenate(attn_parts, axis=0), NT)
    product_ref[...] = (gate * product).astype(jnp.bfloat16)
    query_grad = jnp.transpose(jnp.concatenate(query_parts, axis=0).astype(jnp.bfloat16))
    index = index_ref[...][:, :1].astype(jnp.float32)
    place = index == (iota((slots, rows), 1) + 1).astype(jnp.float32)
    place = jnp.where(place, 1.0, 0.0).astype(jnp.bfloat16)
    back_ref[...] = mm(place, query_grad).astype(jnp.bfloat16)
    return key_term.astype(jnp.bfloat16), value_term.astype(jnp.bfloat16)


def gate_lanes(total, shape):
    high = total.astype(jnp.bfloat16).astype(jnp.float32)
    middle = (total - high).astype(jnp.bfloat16).astype(jnp.float32)
    low = total - high - middle
    lane = iota(shape, 1)
    terms = jnp.where(lane == 0, high, jnp.where(lane == 1, middle, low))
    return jnp.where(lane < 3, terms, 0.0).astype(jnp.bfloat16)


def attention_kernel(blocks, pairs, gate_ref, before_ref, query_ref, weight_ref, rows_ref,
                     rows_t_ref, index_ref, *refs):
    parts, outs = refs[: blocks + 1], refs[blocks + 1 : 2 * blocks + 2]
    product_ref, back_ref, gate_out_ref = refs[2 * blocks + 2 :]
    step = pl.program_id(0)

    @pl.when(step == 0)
    def _():
        gate_out_ref[...] = before_ref[...]

    @pl.when(step < pairs)
    def _():
        chunk = parts[-1].shape[0]
        keys = jnp.concatenate([part[:chunk] for part in parts[:-1]], axis=0)
        values = jnp.concatenate(
            [part[chunk:] for part in parts[:-2]] + [parts[-1][...]], axis=0
        )
        key_term, value_term = attend(
            gate_ref, query_ref, weight_ref, rows_ref, rows_t_ref, index_ref, keys, values,
            product_ref, back_ref, gate_out_ref,
        )
        for number, out in enumerate(outs[:-2]):
            span = slice(number * chunk, (number + 1) * chunk)
            out[:chunk] = key_term[span]
            out[chunk:] = value_term[span]
        outs[-2][...] = key_term[-chunk:]
        outs[-1][...] = value_term[-chunk:]

    @pl.when(step == pairs)
    def _():
        total = jnp.sum(gate_out_ref[...], axis=1, keepdims=True)
        back_ref[...] = gate_lanes(total, back_ref.shape)


def attention(gate_logit, before, queries, out_weight, grad_rows, rows_t, recv, parts, first_pair,
              extra):
    rows, width = queries.shape
    slots = recv.shape[0]
    span = parts[0].shape[1]
    pairs = span // LANES
    tokens = (len(parts) - 1) * parts[-1].shape[0]
    at = lambda i: jnp.minimum(i, pairs - 1)
    columns = lambda i: (0, at(i))
    part_specs = [pl.BlockSpec((part.shape[0], LANES), columns) for part in parts]
    whole = lambda i: (0, 0)
    outs = pl.pallas_call(
        lambda *refs: attention_kernel(len(parts) - 1, pairs, *refs),
        grid=(pairs + extra,),
        out_shape=(
            *[jax.ShapeDtypeStruct(part.shape, jnp.bfloat16) for part in parts],
            jax.ShapeDtypeStruct((width, span), jnp.bfloat16),
            jax.ShapeDtypeStruct((slots, span + extra * LANES), jnp.bfloat16),
            jax.ShapeDtypeStruct((1, rows), jnp.float32),
        ),
        in_specs=[
            pl.BlockSpec(memory_space=pltpu.SMEM),
            pl.BlockSpec((1, rows), whole),
            pl.BlockSpec((rows, LANES), lambda i: (0, at(i) + first_pair)),
            pl.BlockSpec((LANES, width), lambda i: (at(i) + first_pair, 0)),
            pl.BlockSpec((rows, width), whole),
            pl.BlockSpec((width, rows), whole),
            pl.BlockSpec((slots, LANES), lambda i: (0, width // LANES)),
            *part_specs,
        ],
        out_specs=(
            *part_specs,
            pl.BlockSpec((width, LANES), columns),
            pl.BlockSpec((slots, LANES), lambda i: (0, i)),
            pl.BlockSpec((1, rows), whole),
        ),
        compiler_params=params(VMEM_WHOLE),
        name="attention",
        cost_estimate=pl.CostEstimate(
            flops=ATTENTION_COST * rows * tokens * span,
            bytes_accessed=8 * tokens * span + 12 * rows * span,
            transcendentals=rows * tokens * span // HEAD_DIM,
        ),
    )(gate_logit, before, queries, out_weight, grad_rows, rows_t, recv, *parts)
    return outs[: len(parts)], *outs[len(parts) :]


def pick_kernel(pair_cap, target_ref, first_ref, second_ref, out_ref, gate_ref):
    slots, half = first_ref.shape
    target = as_column(target_ref[...].astype(jnp.float32))
    place = target == iota((slots, slots), 1).astype(jnp.float32)
    place = jnp.where(place, 1.0, 0.0).astype(jnp.bfloat16)
    out_ref[:, :half] = mm(place, first_ref[...]).astype(jnp.bfloat16)
    out_ref[:, half:] = mm(place, second_ref[:, :half]).astype(jnp.bfloat16)
    shares = second_ref[:, half:].astype(jnp.float32)
    shares = jnp.where(iota(shares.shape, 0) % pair_cap == 0, shares, 0.0)
    gate_ref[...] = jnp.sum(jnp.sum(shares, axis=0, keepdims=True), axis=1, keepdims=True)


def pick_rows(target, first, second, pair_cap):
    slots, half = first.shape
    vmem = pl.BlockSpec(memory_space=pltpu.VMEM)
    return pl.pallas_call(
        lambda *refs: pick_kernel(pair_cap, *refs),
        out_shape=(
            jax.ShapeDtypeStruct((slots, 2 * half), jnp.bfloat16),
            jax.ShapeDtypeStruct((1, 1), jnp.float32),
        ),
        in_specs=[vmem, vmem, vmem],
        out_specs=(vmem, vmem),
        compiler_params=params(),
        name="pick_rows",
        cost_estimate=pl.CostEstimate(
            flops=4 * slots * slots * half,
            bytes_accessed=8 * slots * half,
            transcendentals=0,
        ),
    )(target, first, second)


def shift(value, step):
    count = lax.axis_size("ctx")
    pairs = [(i, (i + step) % count) for i in range(count)]
    return lax.ppermute(value, "ctx", pairs)


def gather_near(chunk):
    parts = [chunk]
    ahead = behind = chunk
    for _ in range(1, lax.axis_size("ctx") // 2):
        ahead = shift(ahead, 1)
        behind = shift(behind, -1)
        parts += [ahead, behind]
    return parts


def halves_kernel(ahead_ref, behind_ref, keys_ref, values_ref):
    half = keys_ref.shape[0]
    keys_ref[...] = ahead_ref[:half]
    values_ref[...] = behind_ref[half:]


def farthest(ahead, behind, cost):
    half = ahead.shape[0] // 2
    vmem = pl.BlockSpec(memory_space=pltpu.VMEM)
    return pl.pallas_call(
        halves_kernel,
        out_shape=(jax.ShapeDtypeStruct((half, ahead.shape[1]), ahead.dtype),) * 2,
        in_specs=[vmem, vmem],
        out_specs=(vmem, vmem),
        compiler_params=params(),
        name="farthest",
        cost_estimate=pl.CostEstimate(
            flops=cost * ahead.size, bytes_accessed=4 * ahead.size, transcendentals=0
        ),
    )(ahead, behind)


def gather_far(parts, cost):
    keys, values = farthest(parts[-2], parts[-1], cost)
    return [*parts, shift(keys, 1), shift(values, -1)]


def add(left, right):
    return (left.astype(jnp.float32) + right.astype(jnp.float32)).astype(jnp.bfloat16)


def start_sums(parts):
    return shift(parts[-2], -1), shift(parts[-1], 1)


def step_kernel(*refs):
    back_ref, forth_ref = refs[-2:]
    rows = refs[0].shape[0]
    half = rows // 2
    for number in range(2):
        back, forth, far_keys, far_values = refs[4 * number : 4 * number + 4]
        first = number * rows
        middle = first + half
        back_ref[first:middle] = add(back[:half], far_keys[...])
        back_ref[middle : first + rows] = back[half:]
        forth_ref[first:middle] = forth[:half]
        forth_ref[middle : first + rows] = add(forth[half:], far_values[...])


def step_sums(halves):
    vmem = pl.BlockSpec(memory_space=pltpu.VMEM)
    back = halves[0][0]
    shape = jax.ShapeDtypeStruct((2 * back.shape[0], back.shape[1]), back.dtype)
    return pl.pallas_call(
        step_kernel,
        out_shape=(shape, shape),
        in_specs=[vmem] * 8,
        out_specs=(vmem, vmem),
        compiler_params=params(),
        name="step_sums",
        cost_estimate=pl.CostEstimate(
            flops=STEP_COST * back.size, bytes_accessed=16 * back.size, transcendentals=0
        ),
    )(*halves[0], *halves[1])


def total_kernel(first_ref, second_ref, back_ref, forth_ref, key_ref, value_ref):
    rows, span = first_ref.shape
    half = rows // 2
    for number, own_ref in enumerate((first_ref, second_ref)):
        moved = slice(number * rows, (number + 1) * rows)
        total = own_ref[...].astype(jnp.float32) + back_ref[moved].astype(jnp.float32)
        total = (total + forth_ref[moved].astype(jnp.float32)).astype(jnp.bfloat16)
        columns = slice(number * span, (number + 1) * span)
        key_ref[:, columns] = total[:half]
        value_ref[:, columns] = total[half:]


def total_sums(first, second, back, forth):
    vmem = pl.BlockSpec(memory_space=pltpu.VMEM)
    shape = jax.ShapeDtypeStruct((first.shape[0] // 2, 2 * first.shape[1]), first.dtype)
    return pl.pallas_call(
        total_kernel,
        out_shape=(shape, shape),
        in_specs=[vmem] * 4,
        out_specs=(vmem, vmem),
        compiler_params=params(),
        name="total_sums",
        cost_estimate=pl.CostEstimate(
            flops=TOTAL_COST * first.size, bytes_accessed=16 * first.size, transcendentals=0
        ),
    )(first, second, back, forth)


def ring_sums(first_terms, second_terms, first_far, second_far):
    steps = lax.axis_size("ctx") // 2 - 1
    far = 2 * steps - 1
    back, forth = step_sums(
        [
            (terms[far], terms[far + 1], *moved)
            for terms, moved in ((first_terms, first_far), (second_terms, second_far))
        ]
    )
    for step in range(steps, 0, -1):
        if step < steps:
            near = 2 * step - 1
            back, forth = (
                add(jnp.concatenate([first_terms[at], second_terms[at]], axis=0), moved)
                for at, moved in ((near, back), (near + 1, forth))
            )
        back = shift(back, -1)
        forth = shift(forth, 1)
    return total_sums(first_terms[0], second_terms[0], back, forth)


def halve(term, bit, lowest):
    rec_count = lax.axis_size("rec")
    ctx_count, left, rows, width = term.shape
    pair = (left // 2, 2) if lowest else (2, left // 2)
    term = term.reshape(ctx_count, *pair, rows, width)
    mine = (lax.axis_index("rec") >> bit) & 1

    def half(which):
        return lax.dynamic_index_in_dim(term, which, 2 if lowest else 1, keepdims=False)

    got = lax.ppermute(half(1 - mine), "rec", [(i, i ^ (1 << bit)) for i in range(rec_count)])
    return add(half(mine), got)


def sum_blocks(term):
    ctx_count = lax.axis_size("ctx")
    block = lax.axis_index("ctx")
    total = lax.dynamic_index_in_dim(term, block, 0, keepdims=False).astype(jnp.float32)
    for step in range(1, ctx_count):
        sent = lax.dynamic_index_in_dim(term, block ^ step, 0, keepdims=False)
        pairs = [(i, i ^ step) for i in range(ctx_count)]
        total = total + lax.ppermute(sent, "ctx", pairs).astype(jnp.float32)
    return total


def exchange(value, count):
    slots, width = value.shape
    moved = lax.all_to_all(
        value.reshape(count, slots // count, width),
        ("ctx", "rec"),
        split_axis=0,
        concat_axis=0,
        tiled=True,
    )
    return moved.reshape(slots, width)


def local(
    queries,
    video_keys,
    video_values,
    out_weight,
    gate_logit,
    row_grads,
    dest_device,
    dest_row,
    live_count,
):
    count = lax.axis_size("ctx") * lax.axis_size("rec")
    rows, width = queries.shape[1:]
    half = width // 2
    tie = lax.optimization_barrier
    first, second = (
        jnp.concatenate([video_keys[0][:, part], video_values[0][:, part]], axis=0)
        for part in (slice(0, half), slice(half, width))
    )
    first_parts = gather_far(gather_near(first), FAR_COST)
    send, target = route_prep(live_count, dest_device, dest_row, row_grads, count)
    recv = exchange(send, count)
    recv, second = tie((recv, second))
    second_parts = gather_near(second)
    grad_rows, rows_t = unpack_rows(recv, rows)
    common = (queries[0], out_weight, grad_rows, rows_t, recv)
    first_terms, first_product, first_back, gate_part = attention(
        gate_logit, jnp.zeros((1, rows), jnp.float32), *common, first_parts, 0, 0
    )
    first_far = start_sums(first_terms)
    first_returned = exchange(first_back, count)
    second_parts, gate_part = tie((second_parts, gate_part))
    blocks, devices = lax.axis_size("ctx"), lax.axis_size("rec")
    shape = (blocks, devices, width // count, half)
    first_product = halve(first_product.reshape(shape), 0, True)
    second_parts = gather_far(second_parts, 1)
    second_terms, second_product, second_back, _ = attention(
        gate_logit, gate_part, *common, second_parts, half // LANES, 1
    )
    second_far = start_sums(second_terms)
    first_far, second_product, first_returned, first_product = tie(
        (first_far, second_product, first_returned, first_product)
    )
    second_product = halve(second_product.reshape(shape), 0, True)
    second_returned = exchange(second_back, count)
    bit = 1
    while first_product.shape[1] > 1:
        opposite = devices.bit_length() - 1 - bit
        first_product = halve(first_product, bit, True)
        second_product = halve(second_product, opposite, False)
        bit += 1
    weight_chips = jnp.concatenate([first_product[:, 0], second_product[:, 0]], axis=2)
    key_sum, value_sum = ring_sums(first_terms, second_terms, first_far, second_far)
    weight_grad = sum_blocks(weight_chips)
    query_grads, gate_total = pick_rows(
        target, first_returned, second_returned, row_grads.shape[0] // count
    )
    gate_value = jnp.tanh(gate_logit[0])
    gate_grad = (1.0 - gate_value * gate_value) * gate_total[0, 0]
    return query_grads, key_sum[None], value_sum[None], weight_grad, gate_grad.reshape(1)


def solution(mesh):
    in_specs = (
        P("rec", "ctx", None),
        P("rec", "ctx", None),
        P("rec", "ctx", None),
        P(),
        P(),
        P(("ctx", "rec"), None),
        P(("ctx", "rec")),
        P(("ctx", "rec")),
        P(("ctx", "rec")),
    )
    out_specs = (
        P(("ctx", "rec"), None),
        P("rec", "ctx", None),
        P("rec", "ctx", None),
        P(("ctx", "rec"), None),
        P(),
    )
    return jax.shard_map(local, mesh=mesh, in_specs=in_specs, out_specs=out_specs, check_vma=False)
```

```python
import jax
import jax.numpy as jnp
from jax import lax
from jax.experimental import pallas as pl
from jax.experimental.pallas import tpu as pltpu
from jax.sharding import PartitionSpec as P

HEAD_DIM = 64
LANES = 128
VMEM_LIMIT = 32 * 1024 * 1024
VMEM_WHOLE = 62 * 1024 * 1024
ATTENTION_COST = 150
FAR_COST = 300000
STEP_COST = 74000
FIRST_COST = 300000
SECOND_COST = 1000
NT = (((1,), (1,)), ((), ()))
NN = (((1,), (0,)), ((), ()))


def mm(left, right, dims=NN):
    return lax.dot_general(left, right, dims, preferred_element_type=jnp.float32)


def iota(shape, dim):
    return lax.broadcasted_iota(jnp.int32, shape, dim)


def params(limit=VMEM_LIMIT):
    return pltpu.CompilerParams(vmem_limit_bytes=limit)


def as_column(row_vector):
    wide = jnp.broadcast_to(row_vector, (LANES, row_vector.shape[1]))
    return jnp.transpose(wide)[:, :1]


def as_row(column_block):
    return jnp.transpose(column_block.astype(jnp.float32))[:1, :]


def prep_kernel(pair_cap, owners, live_ref, dest_ref, row_ref, grads_ref, send_ref, target_ref):
    slots, width = grads_ref.shape
    slot = iota((1, slots), 1)
    is_live = slot < live_ref[0]
    dest = dest_ref[...]
    hot = jnp.logical_and(iota((owners, slots), 0) == dest, is_live)
    hot_f = jnp.where(hot, 1.0, 0.0)
    earlier = jnp.where(iota((slots, slots), 0) < iota((slots, slots), 1), 1.0, 0.0)
    before = mm(hot_f.astype(jnp.bfloat16), earlier.astype(jnp.bfloat16))
    rank = jnp.sum(hot_f * before, axis=0, keepdims=True).astype(jnp.int32)
    target = jnp.where(is_live, dest * pair_cap + rank, slots)
    target_ref[...] = target
    chosen = iota((slots, slots), 0) == target
    place = jnp.where(chosen, 1.0, 0.0).astype(jnp.bfloat16)
    send_ref[:, :width] = mm(place, grads_ref[...]).astype(jnp.bfloat16)
    row_no = (row_ref[...] + 1).astype(jnp.float32)
    index = jnp.sum(jnp.where(chosen, row_no, 0.0), axis=1, keepdims=True)
    send_ref[:, width:] = jnp.broadcast_to(index, (slots, LANES)).astype(jnp.bfloat16)


def route_prep(live_count, dest_device, dest_row, row_grads, owners):
    slots, width = row_grads.shape
    kernel = lambda *refs: prep_kernel(slots // owners, owners, *refs)
    vmem = pl.BlockSpec(memory_space=pltpu.VMEM)
    return pl.pallas_call(
        kernel,
        out_shape=(
            jax.ShapeDtypeStruct((slots, width + LANES), jnp.bfloat16),
            jax.ShapeDtypeStruct((1, slots), jnp.int32),
        ),
        in_specs=[pl.BlockSpec(memory_space=pltpu.SMEM), vmem, vmem, vmem],
        out_specs=(vmem, vmem),
        compiler_params=params(),
        name="route_prep",
        cost_estimate=pl.CostEstimate(
            flops=2 * slots * slots * width,
            bytes_accessed=4 * slots * width,
            transcendentals=0,
        ),
    )(live_count, dest_device.reshape(1, slots), dest_row.reshape(1, slots), row_grads)


def head_masks(shape, dim):
    first = iota(shape, dim) < HEAD_DIM
    return first, jnp.logical_not(first)


def keep(mask, value):
    return jnp.where(mask, value, jnp.zeros((), value.dtype))


def unpack_kernel(recv_ref, rows_ref, rows_t_ref):
    slots = recv_ref.shape[0]
    rows, width = rows_ref.shape
    index = as_row(recv_ref[:, width:])
    place = index == (iota((rows, slots), 0) + 1).astype(jnp.float32)
    place = jnp.where(place, 1.0, 0.0).astype(jnp.bfloat16)
    owned = mm(place, recv_ref[:, :width]).astype(jnp.bfloat16)
    rows_ref[...] = owned
    rows_t_ref[...] = jnp.transpose(owned)


def unpack_rows(recv, rows):
    slots, width = recv.shape
    width -= LANES
    vmem = pl.BlockSpec(memory_space=pltpu.VMEM)
    return pl.pallas_call(
        unpack_kernel,
        out_shape=(
            jax.ShapeDtypeStruct((rows, width), jnp.bfloat16),
            jax.ShapeDtypeStruct((width, rows), jnp.bfloat16),
        ),
        in_specs=[vmem],
        out_specs=(vmem, vmem),
        compiler_params=params(),
        name="unpack_rows",
        cost_estimate=pl.CostEstimate(
            flops=2 * slots * rows * width,
            bytes_accessed=2 * (slots + 2 * rows) * width,
            transcendentals=0,
        ),
    )(recv)


def attend(gate_ref, query_ref, weight_ref, rows_ref, rows_t_ref, index_ref, keys, values,
           product_ref, back_ref, gate_out_ref):
    rows = query_ref.shape[0]
    slots = index_ref.shape[0]
    root = HEAD_DIM ** -0.5
    query = query_ref[...] * jnp.asarray(root, jnp.bfloat16)
    keys_tr = jnp.transpose(keys)
    values_tr = jnp.transpose(values)
    gate = jnp.tanh(jnp.full((1, LANES), gate_ref[0], jnp.float32))[:, :1]
    upstream = mm(weight_ref[...], rows_ref[...], NT)
    grad_t = (gate * upstream).astype(jnp.bfloat16)
    grad = jnp.transpose(grad_t)
    lane_masks = head_masks((rows, LANES), 1)
    row_masks = head_masks((LANES, rows), 0)
    spans = [slice(head * HEAD_DIM, (head + 1) * HEAD_DIM) for head in range(2)]
    query_h = [keep(mask, query) for mask in lane_masks]
    grad_h = [keep(mask, grad) for mask in lane_masks]
    scores = [mm(keys, part, NT) for part in query_h]
    dprobs = [mm(values, keep(mask, grad_t)) for mask in row_masks]
    probs, low = [], []
    for head in range(2):
        peak = jnp.max(scores[head], axis=0, keepdims=True)
        shifted = jnp.exp(scores[head] - peak)
        inverse = 1.0 / jnp.sum(shifted, axis=0, keepdims=True)
        probs.append(shifted * inverse)
        low.append(probs[head].astype(jnp.bfloat16))
    attn_parts = [mm(values_tr[spans[h], :], low[h]).astype(jnp.bfloat16) for h in range(2)]
    dscores = []
    gate_sum = None
    for head in range(2):
        attn_wide = attn_parts[head].astype(jnp.float32)
        span = spans[head]
        delta = jnp.sum(grad_t[span, :].astype(jnp.float32) * attn_wide, axis=0, keepdims=True)
        gate_h = jnp.sum(upstream[span, :] * attn_wide, axis=0, keepdims=True)
        gate_sum = gate_h if head == 0 else gate_sum + gate_h
        dscores.append((probs[head] * (dprobs[head] - delta)).astype(jnp.bfloat16))
    value_term = mm(low[0], grad_h[0]) + mm(low[1], grad_h[1])
    key_term = mm(dscores[0], query_h[0]) + mm(dscores[1], query_h[1])
    query_parts = [mm(keys_tr[spans[h], :], dscores[h]) * root for h in range(2)]
    gate_out_ref[...] += gate_sum
    product = mm(rows_t_ref[...], jnp.concatenate(attn_parts, axis=0), NT)
    product_ref[...] = (gate * product).astype(jnp.bfloat16)
    query_grad = jnp.transpose(jnp.concatenate(query_parts, axis=0).astype(jnp.bfloat16))
    index = index_ref[...][:, :1].astype(jnp.float32)
    place = index == (iota((slots, rows), 1) + 1).astype(jnp.float32)
    place = jnp.where(place, 1.0, 0.0).astype(jnp.bfloat16)
    back_ref[...] = mm(place, query_grad).astype(jnp.bfloat16)
    return key_term.astype(jnp.bfloat16), value_term.astype(jnp.bfloat16)


def gate_lanes(total, shape):
    high = total.astype(jnp.bfloat16).astype(jnp.float32)
    middle = (total - high).astype(jnp.bfloat16).astype(jnp.float32)
    low = total - high - middle
    lane = iota(shape, 1)
    terms = jnp.where(lane == 0, high, jnp.where(lane == 1, middle, low))
    return jnp.where(lane < 3, terms, 0.0).astype(jnp.bfloat16)


def attention_kernel(blocks, pairs, gate_ref, before_ref, query_ref, weight_ref, rows_ref,
                     rows_t_ref, index_ref, *refs):
    parts, outs = refs[: blocks + 1], refs[blocks + 1 : 2 * blocks + 2]
    product_ref, back_ref, gate_out_ref = refs[2 * blocks + 2 :]
    step = pl.program_id(0)

    @pl.when(step == 0)
    def _():
        gate_out_ref[...] = before_ref[...]

    @pl.when(step < pairs)
    def _():
        chunk = parts[-1].shape[0]
        keys = jnp.concatenate([part[:chunk] for part in parts[:-1]], axis=0)
        values = jnp.concatenate(
            [part[chunk:] for part in parts[:-2]] + [parts[-1][...]], axis=0
        )
        key_term, value_term = attend(
            gate_ref, query_ref, weight_ref, rows_ref, rows_t_ref, index_ref, keys, values,
            product_ref, back_ref, gate_out_ref,
        )
        for number, out in enumerate(outs[:-2]):
            span = slice(number * chunk, (number + 1) * chunk)
            out[:chunk] = key_term[span]
            out[chunk:] = value_term[span]
        outs[-2][...] = key_term[-chunk:]
        outs[-1][...] = value_term[-chunk:]

    @pl.when(step == pairs)
    def _():
        total = jnp.sum(gate_out_ref[...], axis=1, keepdims=True)
        back_ref[...] = gate_lanes(total, back_ref.shape)


def attention(gate_logit, before, queries, out_weight, grad_rows, rows_t, recv, parts, first_pair,
              extra):
    rows, width = queries.shape
    slots = recv.shape[0]
    span = parts[0].shape[1]
    pairs = span // LANES
    tokens = (len(parts) - 1) * parts[-1].shape[0]
    at = lambda i: jnp.minimum(i, pairs - 1)
    columns = lambda i: (0, at(i))
    part_specs = [pl.BlockSpec((part.shape[0], LANES), columns) for part in parts]
    whole = lambda i: (0, 0)
    outs = pl.pallas_call(
        lambda *refs: attention_kernel(len(parts) - 1, pairs, *refs),
        grid=(pairs + extra,),
        out_shape=(
            *[jax.ShapeDtypeStruct(part.shape, jnp.bfloat16) for part in parts],
            jax.ShapeDtypeStruct((width, span), jnp.bfloat16),
            jax.ShapeDtypeStruct((slots, span + extra * LANES), jnp.bfloat16),
            jax.ShapeDtypeStruct((1, rows), jnp.float32),
        ),
        in_specs=[
            pl.BlockSpec(memory_space=pltpu.SMEM),
            pl.BlockSpec((1, rows), whole),
            pl.BlockSpec((rows, LANES), lambda i: (0, at(i) + first_pair)),
            pl.BlockSpec((LANES, width), lambda i: (at(i) + first_pair, 0)),
            pl.BlockSpec((rows, width), whole),
            pl.BlockSpec((width, rows), whole),
            pl.BlockSpec((slots, LANES), lambda i: (0, width // LANES)),
            *part_specs,
        ],
        out_specs=(
            *part_specs,
            pl.BlockSpec((width, LANES), columns),
            pl.BlockSpec((slots, LANES), lambda i: (0, i)),
            pl.BlockSpec((1, rows), whole),
        ),
        compiler_params=params(VMEM_WHOLE),
        name="attention",
        cost_estimate=pl.CostEstimate(
            flops=ATTENTION_COST * rows * tokens * span,
            bytes_accessed=8 * tokens * span + 12 * rows * span,
            transcendentals=rows * tokens * span // HEAD_DIM,
        ),
    )(gate_logit, before, queries, out_weight, grad_rows, rows_t, recv, *parts)
    return outs[: len(parts)], *outs[len(parts) :]


def pick_kernel(pair_cap, target_ref, first_ref, second_ref, out_ref, gate_ref):
    slots, half = first_ref.shape
    target = as_column(target_ref[...].astype(jnp.float32))
    place = target == iota((slots, slots), 1).astype(jnp.float32)
    place = jnp.where(place, 1.0, 0.0).astype(jnp.bfloat16)
    out_ref[:, :half] = mm(place, first_ref[...]).astype(jnp.bfloat16)
    out_ref[:, half:] = mm(place, second_ref[:, :half]).astype(jnp.bfloat16)
    shares = second_ref[:, half:].astype(jnp.float32)
    shares = jnp.where(iota(shares.shape, 0) % pair_cap == 0, shares, 0.0)
    gate_ref[...] = jnp.sum(jnp.sum(shares, axis=0, keepdims=True), axis=1, keepdims=True)


def pick_rows(target, first, second, pair_cap):
    slots, half = first.shape
    vmem = pl.BlockSpec(memory_space=pltpu.VMEM)
    return pl.pallas_call(
        lambda *refs: pick_kernel(pair_cap, *refs),
        out_shape=(
            jax.ShapeDtypeStruct((slots, 2 * half), jnp.bfloat16),
            jax.ShapeDtypeStruct((1, 1), jnp.float32),
        ),
        in_specs=[vmem, vmem, vmem],
        out_specs=(vmem, vmem),
        compiler_params=params(),
        name="pick_rows",
        cost_estimate=pl.CostEstimate(
            flops=4 * slots * slots * half,
            bytes_accessed=8 * slots * half,
            transcendentals=0,
        ),
    )(target, first, second)


def shift(value, step):
    count = lax.axis_size("ctx")
    pairs = [(i, (i + step) % count) for i in range(count)]
    return lax.ppermute(value, "ctx", pairs)


def gather_near(chunk):
    parts = [chunk]
    ahead = behind = chunk
    for _ in range(1, lax.axis_size("ctx") // 2):
        ahead = shift(ahead, 1)
        behind = shift(behind, -1)
        parts += [ahead, behind]
    return parts


def halves_kernel(ahead_ref, behind_ref, keys_ref, values_ref):
    half = keys_ref.shape[0]
    keys_ref[...] = ahead_ref[:half]
    values_ref[...] = behind_ref[half:]


def farthest(ahead, behind, cost):
    half = ahead.shape[0] // 2
    vmem = pl.BlockSpec(memory_space=pltpu.VMEM)
    return pl.pallas_call(
        halves_kernel,
        out_shape=(jax.ShapeDtypeStruct((half, ahead.shape[1]), ahead.dtype),) * 2,
        in_specs=[vmem, vmem],
        out_specs=(vmem, vmem),
        compiler_params=params(),
        name="farthest",
        cost_estimate=pl.CostEstimate(
            flops=cost * ahead.size, bytes_accessed=4 * ahead.size, transcendentals=0
        ),
    )(ahead, behind)


def gather_far(parts, cost):
    keys, values = farthest(parts[-2], parts[-1], cost)
    return [*parts, shift(keys, 1), shift(values, -1)]


def add(left, right):
    return (left.astype(jnp.float32) + right.astype(jnp.float32)).astype(jnp.bfloat16)


def start_sums(parts):
    return shift(parts[-2], -1), shift(parts[-1], 1)


def step_kernel(back_ref, forth_ref, far_keys_ref, far_values_ref, back_out_ref, forth_out_ref):
    half = far_keys_ref.shape[0]
    back_out_ref[:half] = add(back_ref[:half], far_keys_ref[...])
    back_out_ref[half:] = back_ref[half:]
    forth_out_ref[:half] = forth_ref[:half]
    forth_out_ref[half:] = add(forth_ref[half:], far_values_ref[...])


def step_sums(back, forth, far_keys, far_values):
    vmem = pl.BlockSpec(memory_space=pltpu.VMEM)
    return pl.pallas_call(
        step_kernel,
        out_shape=(jax.ShapeDtypeStruct(back.shape, back.dtype),) * 2,
        in_specs=[vmem] * 4,
        out_specs=(vmem, vmem),
        compiler_params=params(),
        name="step_sums",
        cost_estimate=pl.CostEstimate(
            flops=STEP_COST * back.size,
            bytes_accessed=8 * back.size,
            transcendentals=0,
        ),
    )(back, forth, far_keys, far_values)


def send_sums(parts, far_keys, far_values):
    steps = lax.axis_size("ctx") // 2 - 1
    back, forth = step_sums(parts[2 * steps - 1], parts[2 * steps], far_keys, far_values)
    for step in range(steps, 0, -1):
        if step < steps:
            back = add(parts[2 * step - 1], back)
            forth = add(parts[2 * step], forth)
        back = shift(back, -1)
        forth = shift(forth, 1)
    return parts[0], back, forth


def total_kernel(own_ref, back_ref, forth_ref, *refs):
    total = own_ref[...].astype(jnp.float32) + back_ref[...].astype(jnp.float32)
    total = (total + forth_ref[...].astype(jnp.float32)).astype(jnp.bfloat16)
    outs = refs[-2:]
    half = outs[0].shape[0]
    span = total.shape[1]
    for before, out, value in zip(refs[:-2] or (None, None), outs, (total[:half], total[half:])):
        if before is not None:
            out[:, :-span] = before[...]
        out[:, -span:] = value


def total_sums(own, back, forth, before, cost):
    vmem = pl.BlockSpec(memory_space=pltpu.VMEM)
    span = own.shape[1] + (before[0].shape[1] if before else 0)
    shape = jax.ShapeDtypeStruct((own.shape[0] // 2, span), own.dtype)
    return pl.pallas_call(
        total_kernel,
        out_shape=(shape, shape),
        in_specs=[vmem] * (3 + len(before)),
        out_specs=(vmem, vmem),
        compiler_params=params(),
        name="total_sums",
        cost_estimate=pl.CostEstimate(
            flops=cost * own.size, bytes_accessed=8 * own.size, transcendentals=0
        ),
    )(own, back, forth, *before)


def halve(term, bit, lowest):
    rec_count = lax.axis_size("rec")
    ctx_count, left, rows, width = term.shape
    pair = (left // 2, 2) if lowest else (2, left // 2)
    term = term.reshape(ctx_count, *pair, rows, width)
    mine = (lax.axis_index("rec") >> bit) & 1

    def half(which):
        return lax.dynamic_index_in_dim(term, which, 2 if lowest else 1, keepdims=False)

    got = lax.ppermute(half(1 - mine), "rec", [(i, i ^ (1 << bit)) for i in range(rec_count)])
    return add(half(mine), got)


def sum_blocks(term):
    ctx_count = lax.axis_size("ctx")
    block = lax.axis_index("ctx")
    total = lax.dynamic_index_in_dim(term, block, 0, keepdims=False).astype(jnp.float32)
    for step in range(1, ctx_count):
        sent = lax.dynamic_index_in_dim(term, block ^ step, 0, keepdims=False)
        pairs = [(i, i ^ step) for i in range(ctx_count)]
        total = total + lax.ppermute(sent, "ctx", pairs).astype(jnp.float32)
    return total


def exchange(value, count):
    slots, width = value.shape
    moved = lax.all_to_all(
        value.reshape(count, slots // count, width),
        ("ctx", "rec"),
        split_axis=0,
        concat_axis=0,
        tiled=True,
    )
    return moved.reshape(slots, width)


def local(
    queries,
    video_keys,
    video_values,
    out_weight,
    gate_logit,
    row_grads,
    dest_device,
    dest_row,
    live_count,
):
    count = lax.axis_size("ctx") * lax.axis_size("rec")
    rows, width = queries.shape[1:]
    half = width // 2
    tie = lax.optimization_barrier
    first, second = (
        jnp.concatenate([video_keys[0][:, part], video_values[0][:, part]], axis=0)
        for part in (slice(0, half), slice(half, width))
    )
    first_parts = gather_far(gather_near(first), FAR_COST)
    send, target = route_prep(live_count, dest_device, dest_row, row_grads, count)
    recv = exchange(send, count)
    recv, second = tie((recv, second))
    second_parts = gather_near(second)
    grad_rows, rows_t = unpack_rows(recv, rows)
    common = (queries[0], out_weight, grad_rows, rows_t, recv)
    first_terms, first_product, first_back, gate_part = attention(
        gate_logit, jnp.zeros((1, rows), jnp.float32), *common, first_parts, 0, 0
    )
    first_far = start_sums(first_terms)
    first_returned = exchange(first_back, count)
    second_parts, gate_part = tie((second_parts, gate_part))
    blocks, devices = lax.axis_size("ctx"), lax.axis_size("rec")
    shape = (blocks, devices, width // count, half)
    first_product = halve(first_product.reshape(shape), 0, True)
    second_parts = gather_far(second_parts, 1)
    second_terms, second_product, second_back, _ = attention(
        gate_logit, gate_part, *common, second_parts, half // LANES, 1
    )
    second_far = start_sums(second_terms)
    first_far, second_product, first_returned, first_product = tie(
        (first_far, second_product, first_returned, first_product)
    )
    second_product = halve(second_product.reshape(shape), 0, True)
    second_returned = exchange(second_back, count)
    bit = 1
    while first_product.shape[1] > 1:
        opposite = devices.bit_length() - 1 - bit
        first_product = halve(first_product, bit, True)
        second_product = halve(second_product, opposite, False)
        bit += 1
    weight_chips = jnp.concatenate([first_product[:, 0], second_product[:, 0]], axis=2)
    first_sum = total_sums(*send_sums(first_terms, *first_far), (), FIRST_COST)
    key_sum, value_sum = total_sums(
        *send_sums(second_terms, *second_far), first_sum, SECOND_COST
    )
    weight_grad = sum_blocks(weight_chips)
    query_grads, gate_total = pick_rows(
        target, first_returned, second_returned, row_grads.shape[0] // count
    )
    gate_value = jnp.tanh(gate_logit[0])
    gate_grad = (1.0 - gate_value * gate_value) * gate_total[0, 0]
    return query_grads, key_sum[None], value_sum[None], weight_grad, gate_grad.reshape(1)


def solution(mesh):
    in_specs = (
        P("rec", "ctx", None),
        P("rec", "ctx", None),
        P("rec", "ctx", None),
        P(),
        P(),
        P(("ctx", "rec"), None),
        P(("ctx", "rec")),
        P(("ctx", "rec")),
        P(("ctx", "rec")),
    )
    out_specs = (
        P(("ctx", "rec"), None),
        P("rec", "ctx", None),
        P("rec", "ctx", None),
        P(("ctx", "rec"), None),
        P(),
    )
    return jax.shard_map(local, mesh=mesh, in_specs=in_specs, out_specs=out_specs, check_vma=False)
```

```python
import jax
import jax.numpy as jnp
from jax import lax
from jax.experimental import pallas as pl
from jax.experimental.pallas import tpu as pltpu
from jax.sharding import PartitionSpec as P

HEAD_DIM = 64
LANES = 128
VMEM_LIMIT = 32 * 1024 * 1024
VMEM_WHOLE = 62 * 1024 * 1024
ATTENTION_COST = 150
FAR_COST = 300000
STEP_COST = 74000
FIRST_COST = 300000
SECOND_COST = 1000
NT = (((1,), (1,)), ((), ()))
NN = (((1,), (0,)), ((), ()))


def mm(left, right, dims=NN):
    return lax.dot_general(left, right, dims, preferred_element_type=jnp.float32)


def iota(shape, dim):
    return lax.broadcasted_iota(jnp.int32, shape, dim)


def params(limit=VMEM_LIMIT):
    return pltpu.CompilerParams(vmem_limit_bytes=limit)


def as_column(row_vector):
    wide = jnp.broadcast_to(row_vector, (LANES, row_vector.shape[1]))
    return jnp.transpose(wide)[:, :1]


def as_row(column_block):
    return jnp.transpose(column_block.astype(jnp.float32))[:1, :]


def prep_kernel(pair_cap, owners, live_ref, dest_ref, row_ref, grads_ref, send_ref, target_ref):
    slots, width = grads_ref.shape
    slot = iota((1, slots), 1)
    is_live = slot < live_ref[0]
    dest = dest_ref[...]
    hot = jnp.logical_and(iota((owners, slots), 0) == dest, is_live)
    hot_f = jnp.where(hot, 1.0, 0.0)
    earlier = jnp.where(iota((slots, slots), 0) < iota((slots, slots), 1), 1.0, 0.0)
    before = mm(hot_f.astype(jnp.bfloat16), earlier.astype(jnp.bfloat16))
    rank = jnp.sum(hot_f * before, axis=0, keepdims=True).astype(jnp.int32)
    target = jnp.where(is_live, dest * pair_cap + rank, slots)
    target_ref[...] = target
    chosen = iota((slots, slots), 0) == target
    place = jnp.where(chosen, 1.0, 0.0).astype(jnp.bfloat16)
    send_ref[:, :width] = mm(place, grads_ref[...]).astype(jnp.bfloat16)
    row_no = (row_ref[...] + 1).astype(jnp.float32)
    index = jnp.sum(jnp.where(chosen, row_no, 0.0), axis=1, keepdims=True)
    send_ref[:, width:] = jnp.broadcast_to(index, (slots, LANES)).astype(jnp.bfloat16)


def route_prep(live_count, dest_device, dest_row, row_grads, owners):
    slots, width = row_grads.shape
    kernel = lambda *refs: prep_kernel(slots // owners, owners, *refs)
    vmem = pl.BlockSpec(memory_space=pltpu.VMEM)
    return pl.pallas_call(
        kernel,
        out_shape=(
            jax.ShapeDtypeStruct((slots, width + LANES), jnp.bfloat16),
            jax.ShapeDtypeStruct((1, slots), jnp.int32),
        ),
        in_specs=[pl.BlockSpec(memory_space=pltpu.SMEM), vmem, vmem, vmem],
        out_specs=(vmem, vmem),
        compiler_params=params(),
        name="route_prep",
        cost_estimate=pl.CostEstimate(
            flops=2 * slots * slots * width,
            bytes_accessed=4 * slots * width,
            transcendentals=0,
        ),
    )(live_count, dest_device.reshape(1, slots), dest_row.reshape(1, slots), row_grads)


def head_masks(shape, dim):
    first = iota(shape, dim) < HEAD_DIM
    return first, jnp.logical_not(first)


def keep(mask, value):
    return jnp.where(mask, value, jnp.zeros((), value.dtype))


def unpack_kernel(recv_ref, rows_ref, rows_t_ref):
    slots = recv_ref.shape[0]
    rows, width = rows_ref.shape
    index = as_row(recv_ref[:, width:])
    place = index == (iota((rows, slots), 0) + 1).astype(jnp.float32)
    place = jnp.where(place, 1.0, 0.0).astype(jnp.bfloat16)
    owned = mm(place, recv_ref[:, :width]).astype(jnp.bfloat16)
    rows_ref[...] = owned
    rows_t_ref[...] = jnp.transpose(owned)


def unpack_rows(recv, rows):
    slots, width = recv.shape
    width -= LANES
    vmem = pl.BlockSpec(memory_space=pltpu.VMEM)
    return pl.pallas_call(
        unpack_kernel,
        out_shape=(
            jax.ShapeDtypeStruct((rows, width), jnp.bfloat16),
            jax.ShapeDtypeStruct((width, rows), jnp.bfloat16),
        ),
        in_specs=[vmem],
        out_specs=(vmem, vmem),
        compiler_params=params(),
        name="unpack_rows",
        cost_estimate=pl.CostEstimate(
            flops=2 * slots * rows * width,
            bytes_accessed=2 * (slots + 2 * rows) * width,
            transcendentals=0,
        ),
    )(recv)


def attend(gate_ref, query_ref, weight_ref, rows_ref, rows_t_ref, index_ref, keys, values,
           product_ref, back_ref, gate_out_ref):
    rows = query_ref.shape[0]
    slots = index_ref.shape[0]
    root = HEAD_DIM ** -0.5
    query = query_ref[...] * jnp.asarray(root, jnp.bfloat16)
    keys_tr = jnp.transpose(keys)
    values_tr = jnp.transpose(values)
    gate = jnp.tanh(jnp.full((1, LANES), gate_ref[0], jnp.float32))[:, :1]
    upstream = mm(weight_ref[...], rows_ref[...], NT)
    grad_t = (gate * upstream).astype(jnp.bfloat16)
    grad = jnp.transpose(grad_t)
    lane_masks = head_masks((rows, LANES), 1)
    row_masks = head_masks((LANES, rows), 0)
    spans = [slice(head * HEAD_DIM, (head + 1) * HEAD_DIM) for head in range(2)]
    query_h = [keep(mask, query) for mask in lane_masks]
    grad_h = [keep(mask, grad) for mask in lane_masks]
    scores = [mm(keys, part, NT) for part in query_h]
    dprobs = [mm(values, keep(mask, grad_t)) for mask in row_masks]
    probs, low = [], []
    for head in range(2):
        peak = jnp.max(scores[head], axis=0, keepdims=True)
        shifted = jnp.exp(scores[head] - peak)
        inverse = 1.0 / jnp.sum(shifted, axis=0, keepdims=True)
        probs.append(shifted * inverse)
        low.append(probs[head].astype(jnp.bfloat16))
    attn_parts = [mm(values_tr[spans[h], :], low[h]).astype(jnp.bfloat16) for h in range(2)]
    dscores = []
    gate_sum = None
    for head in range(2):
        attn_wide = attn_parts[head].astype(jnp.float32)
        span = spans[head]
        delta = jnp.sum(grad_t[span, :].astype(jnp.float32) * attn_wide, axis=0, keepdims=True)
        gate_h = jnp.sum(upstream[span, :] * attn_wide, axis=0, keepdims=True)
        gate_sum = gate_h if head == 0 else gate_sum + gate_h
        dscores.append((probs[head] * (dprobs[head] - delta)).astype(jnp.bfloat16))
    value_term = mm(low[0], grad_h[0]) + mm(low[1], grad_h[1])
    key_term = mm(dscores[0], query_h[0]) + mm(dscores[1], query_h[1])
    query_parts = [mm(keys_tr[spans[h], :], dscores[h]) * root for h in range(2)]
    gate_out_ref[...] += gate_sum
    product = mm(rows_t_ref[...], jnp.concatenate(attn_parts, axis=0), NT)
    product_ref[...] = (gate * product).astype(jnp.bfloat16)
    query_grad = jnp.transpose(jnp.concatenate(query_parts, axis=0).astype(jnp.bfloat16))
    index = index_ref[...][:, :1].astype(jnp.float32)
    place = index == (iota((slots, rows), 1) + 1).astype(jnp.float32)
    place = jnp.where(place, 1.0, 0.0).astype(jnp.bfloat16)
    back_ref[...] = mm(place, query_grad).astype(jnp.bfloat16)
    return key_term.astype(jnp.bfloat16), value_term.astype(jnp.bfloat16)


def gate_lanes(total, shape):
    high = total.astype(jnp.bfloat16).astype(jnp.float32)
    middle = (total - high).astype(jnp.bfloat16).astype(jnp.float32)
    low = total - high - middle
    lane = iota(shape, 1)
    terms = jnp.where(lane == 0, high, jnp.where(lane == 1, middle, low))
    return jnp.where(lane < 3, terms, 0.0).astype(jnp.bfloat16)


def attention_kernel(blocks, pairs, gate_ref, before_ref, query_ref, weight_ref, rows_ref,
                     rows_t_ref, index_ref, *refs):
    parts, outs = refs[: blocks + 1], refs[blocks + 1 : 2 * blocks + 2]
    product_ref, back_ref, gate_out_ref = refs[2 * blocks + 2 :]
    step = pl.program_id(0)

    @pl.when(step == 0)
    def _():
        gate_out_ref[...] = before_ref[...]

    @pl.when(step < pairs)
    def _():
        chunk = parts[-1].shape[0]
        keys = jnp.concatenate([part[:chunk] for part in parts[:-1]], axis=0)
        values = jnp.concatenate(
            [part[chunk:] for part in parts[:-2]] + [parts[-1][...]], axis=0
        )
        key_term, value_term = attend(
            gate_ref, query_ref, weight_ref, rows_ref, rows_t_ref, index_ref, keys, values,
            product_ref, back_ref, gate_out_ref,
        )
        for number, out in enumerate(outs[:-2]):
            span = slice(number * chunk, (number + 1) * chunk)
            out[:chunk] = key_term[span]
            out[chunk:] = value_term[span]
        outs[-2][...] = key_term[-chunk:]
        outs[-1][...] = value_term[-chunk:]

    @pl.when(step == pairs)
    def _():
        total = jnp.sum(gate_out_ref[...], axis=1, keepdims=True)
        back_ref[...] = gate_lanes(total, back_ref.shape)


def attention(gate_logit, before, queries, out_weight, grad_rows, rows_t, recv, parts, first_pair,
              extra):
    rows, width = queries.shape
    slots = recv.shape[0]
    span = parts[0].shape[1]
    pairs = span // LANES
    tokens = (len(parts) - 1) * parts[-1].shape[0]
    at = lambda i: jnp.minimum(i, pairs - 1)
    columns = lambda i: (0, at(i))
    part_specs = [pl.BlockSpec((part.shape[0], LANES), columns) for part in parts]
    whole = lambda i: (0, 0)
    outs = pl.pallas_call(
        lambda *refs: attention_kernel(len(parts) - 1, pairs, *refs),
        grid=(pairs + extra,),
        out_shape=(
            *[jax.ShapeDtypeStruct(part.shape, jnp.bfloat16) for part in parts],
            jax.ShapeDtypeStruct((width, span), jnp.bfloat16),
            jax.ShapeDtypeStruct((slots, span + extra * LANES), jnp.bfloat16),
            jax.ShapeDtypeStruct((1, rows), jnp.float32),
        ),
        in_specs=[
            pl.BlockSpec(memory_space=pltpu.SMEM),
            pl.BlockSpec((1, rows), whole),
            pl.BlockSpec((rows, LANES), lambda i: (0, at(i) + first_pair)),
            pl.BlockSpec((LANES, width), lambda i: (at(i) + first_pair, 0)),
            pl.BlockSpec((rows, width), whole),
            pl.BlockSpec((width, rows), whole),
            pl.BlockSpec((slots, LANES), lambda i: (0, width // LANES)),
            *part_specs,
        ],
        out_specs=(
            *part_specs,
            pl.BlockSpec((width, LANES), columns),
            pl.BlockSpec((slots, LANES), lambda i: (0, i)),
            pl.BlockSpec((1, rows), whole),
        ),
        compiler_params=params(VMEM_WHOLE),
        name="attention",
        cost_estimate=pl.CostEstimate(
            flops=ATTENTION_COST * rows * tokens * span,
            bytes_accessed=8 * tokens * span + 12 * rows * span,
            transcendentals=rows * tokens * span // HEAD_DIM,
        ),
    )(gate_logit, before, queries, out_weight, grad_rows, rows_t, recv, *parts)
    return outs[: len(parts)], *outs[len(parts) :]


def picked(target_ref, returned):
    slots = returned.shape[0]
    target = as_column(target_ref[...].astype(jnp.float32))
    place = target == iota((slots, slots), 1).astype(jnp.float32)
    place = jnp.where(place, 1.0, 0.0).astype(jnp.bfloat16)
    return mm(place, returned).astype(jnp.bfloat16)


def pick_first_kernel(target_ref, first_ref, out_ref):
    out_ref[...] = picked(target_ref, first_ref[...])


def pick_second_kernel(pair_cap, target_ref, second_ref, _, out_ref, gate_ref):
    half = out_ref.shape[1]
    out_ref[...] = picked(target_ref, second_ref[:, :half])
    shares = second_ref[:, half:].astype(jnp.float32)
    shares = jnp.where(iota(shares.shape, 0) % pair_cap == 0, shares, 0.0)
    gate_ref[...] = jnp.sum(jnp.sum(shares, axis=0, keepdims=True), axis=1, keepdims=True)


def pick_rows(target, first, second, pair_cap):
    slots, half = first.shape
    whole = lambda i: (0, 0)
    shape = jax.ShapeDtypeStruct((slots, 2 * half), jnp.bfloat16)
    cost = pl.CostEstimate(
        flops=2 * slots * slots * half, bytes_accessed=4 * slots * half, transcendentals=0
    )
    left = pl.pallas_call(
        pick_first_kernel,
        grid=(1,),
        out_shape=shape,
        in_specs=[pl.BlockSpec((1, slots), whole), pl.BlockSpec((slots, half), whole)],
        out_specs=pl.BlockSpec((slots, half), whole),
        compiler_params=params(),
        name="pick_first",
        cost_estimate=cost,
    )(target, first)
    return pl.pallas_call(
        lambda *refs: pick_second_kernel(pair_cap, *refs),
        grid=(1,),
        out_shape=(shape, jax.ShapeDtypeStruct((1, 1), jnp.float32)),
        in_specs=[
            pl.BlockSpec((1, slots), whole),
            pl.BlockSpec(second.shape, whole),
            pl.BlockSpec(memory_space=pl.ANY),
        ],
        out_specs=(pl.BlockSpec((slots, half), lambda i: (0, 1)), pl.BlockSpec((1, 1), whole)),
        input_output_aliases={2: 0},
        compiler_params=params(),
        name="pick_second",
        cost_estimate=cost,
    )(target, second, left)


def shift(value, step):
    count = lax.axis_size("ctx")
    pairs = [(i, (i + step) % count) for i in range(count)]
    return lax.ppermute(value, "ctx", pairs)


def gather_near(chunk):
    parts = [chunk]
    ahead = behind = chunk
    for _ in range(1, lax.axis_size("ctx") // 2):
        ahead = shift(ahead, 1)
        behind = shift(behind, -1)
        parts += [ahead, behind]
    return parts


def halves_kernel(ahead_ref, behind_ref, keys_ref, values_ref):
    half = keys_ref.shape[0]
    keys_ref[...] = ahead_ref[:half]
    values_ref[...] = behind_ref[half:]


def farthest(ahead, behind, cost):
    half = ahead.shape[0] // 2
    vmem = pl.BlockSpec(memory_space=pltpu.VMEM)
    return pl.pallas_call(
        halves_kernel,
        out_shape=(jax.ShapeDtypeStruct((half, ahead.shape[1]), ahead.dtype),) * 2,
        in_specs=[vmem, vmem],
        out_specs=(vmem, vmem),
        compiler_params=params(),
        name="farthest",
        cost_estimate=pl.CostEstimate(
            flops=cost * ahead.size, bytes_accessed=4 * ahead.size, transcendentals=0
        ),
    )(ahead, behind)


def gather_far(parts, cost):
    keys, values = farthest(parts[-2], parts[-1], cost)
    return [*parts, shift(keys, 1), shift(values, -1)]


def add(left, right):
    return (left.astype(jnp.float32) + right.astype(jnp.float32)).astype(jnp.bfloat16)


def start_sums(parts):
    return shift(parts[-2], -1), shift(parts[-1], 1)


def step_kernel(back_ref, forth_ref, far_keys_ref, far_values_ref, back_out_ref, forth_out_ref):
    half = far_keys_ref.shape[0]
    back_out_ref[:half] = add(back_ref[:half], far_keys_ref[...])
    back_out_ref[half:] = back_ref[half:]
    forth_out_ref[:half] = forth_ref[:half]
    forth_out_ref[half:] = add(forth_ref[half:], far_values_ref[...])


def step_sums(back, forth, far_keys, far_values):
    vmem = pl.BlockSpec(memory_space=pltpu.VMEM)
    return pl.pallas_call(
        step_kernel,
        out_shape=(jax.ShapeDtypeStruct(back.shape, back.dtype),) * 2,
        in_specs=[vmem] * 4,
        out_specs=(vmem, vmem),
        compiler_params=params(),
        name="step_sums",
        cost_estimate=pl.CostEstimate(
            flops=STEP_COST * back.size,
            bytes_accessed=8 * back.size,
            transcendentals=0,
        ),
    )(back, forth, far_keys, far_values)


def send_sums(parts, far_keys, far_values):
    steps = lax.axis_size("ctx") // 2 - 1
    back, forth = step_sums(parts[2 * steps - 1], parts[2 * steps], far_keys, far_values)
    for step in range(steps, 0, -1):
        if step < steps:
            back = add(parts[2 * step - 1], back)
            forth = add(parts[2 * step], forth)
        back = shift(back, -1)
        forth = shift(forth, 1)
    return parts[0], back, forth


def total_kernel(own_ref, back_ref, forth_ref, *refs):
    total = own_ref[...].astype(jnp.float32) + back_ref[...].astype(jnp.float32)
    total = (total + forth_ref[...].astype(jnp.float32)).astype(jnp.bfloat16)
    outs = refs[-2:]
    half = outs[0].shape[0]
    span = total.shape[1]
    for before, out, value in zip(refs[:-2] or (None, None), outs, (total[:half], total[half:])):
        if before is not None:
            out[:, :-span] = before[...]
        out[:, -span:] = value


def total_sums(own, back, forth, before, cost):
    vmem = pl.BlockSpec(memory_space=pltpu.VMEM)
    span = own.shape[1] + (before[0].shape[1] if before else 0)
    shape = jax.ShapeDtypeStruct((own.shape[0] // 2, span), own.dtype)
    return pl.pallas_call(
        total_kernel,
        out_shape=(shape, shape),
        in_specs=[vmem] * (3 + len(before)),
        out_specs=(vmem, vmem),
        compiler_params=params(),
        name="total_sums",
        cost_estimate=pl.CostEstimate(
            flops=cost * own.size, bytes_accessed=8 * own.size, transcendentals=0
        ),
    )(own, back, forth, *before)


def halve(term, bit, lowest):
    rec_count = lax.axis_size("rec")
    ctx_count, left, rows, width = term.shape
    pair = (left // 2, 2) if lowest else (2, left // 2)
    term = term.reshape(ctx_count, *pair, rows, width)
    mine = (lax.axis_index("rec") >> bit) & 1

    def half(which):
        return lax.dynamic_index_in_dim(term, which, 2 if lowest else 1, keepdims=False)

    got = lax.ppermute(half(1 - mine), "rec", [(i, i ^ (1 << bit)) for i in range(rec_count)])
    return add(half(mine), got)


def sum_blocks(term):
    ctx_count = lax.axis_size("ctx")
    block = lax.axis_index("ctx")
    total = lax.dynamic_index_in_dim(term, block, 0, keepdims=False).astype(jnp.float32)
    for step in range(1, ctx_count):
        sent = lax.dynamic_index_in_dim(term, block ^ step, 0, keepdims=False)
        pairs = [(i, i ^ step) for i in range(ctx_count)]
        total = total + lax.ppermute(sent, "ctx", pairs).astype(jnp.float32)
    return total


def exchange(value, count):
    slots, width = value.shape
    moved = lax.all_to_all(
        value.reshape(count, slots // count, width),
        ("ctx", "rec"),
        split_axis=0,
        concat_axis=0,
        tiled=True,
    )
    return moved.reshape(slots, width)


def local(
    queries,
    video_keys,
    video_values,
    out_weight,
    gate_logit,
    row_grads,
    dest_device,
    dest_row,
    live_count,
):
    count = lax.axis_size("ctx") * lax.axis_size("rec")
    rows, width = queries.shape[1:]
    half = width // 2
    tie = lax.optimization_barrier
    first, second = (
        jnp.concatenate([video_keys[0][:, part], video_values[0][:, part]], axis=0)
        for part in (slice(0, half), slice(half, width))
    )
    first_parts = gather_far(gather_near(first), FAR_COST)
    send, target = route_prep(live_count, dest_device, dest_row, row_grads, count)
    recv = exchange(send, count)
    recv, second = tie((recv, second))
    second_parts = gather_near(second)
    grad_rows, rows_t = unpack_rows(recv, rows)
    common = (queries[0], out_weight, grad_rows, rows_t, recv)
    first_terms, first_product, first_back, gate_part = attention(
        gate_logit, jnp.zeros((1, rows), jnp.float32), *common, first_parts, 0, 0
    )
    first_far = start_sums(first_terms)
    first_returned = exchange(first_back, count)
    second_parts, gate_part = tie((second_parts, gate_part))
    blocks, devices = lax.axis_size("ctx"), lax.axis_size("rec")
    shape = (blocks, devices, width // count, half)
    first_product = halve(first_product.reshape(shape), 0, True)
    second_parts = gather_far(second_parts, 1)
    second_terms, second_product, second_back, _ = attention(
        gate_logit, gate_part, *common, second_parts, half // LANES, 1
    )
    second_far = start_sums(second_terms)
    first_far, second_product, first_returned, first_product = tie(
        (first_far, second_product, first_returned, first_product)
    )
    second_product = halve(second_product.reshape(shape), 0, True)
    second_returned = exchange(second_back, count)
    bit = 1
    while first_product.shape[1] > 1:
        opposite = devices.bit_length() - 1 - bit
        first_product = halve(first_product, bit, True)
        second_product = halve(second_product, opposite, False)
        bit += 1
    weight_chips = jnp.concatenate([first_product[:, 0], second_product[:, 0]], axis=2)
    first_sum = total_sums(*send_sums(first_terms, *first_far), (), FIRST_COST)
    key_sum, value_sum = total_sums(
        *send_sums(second_terms, *second_far), first_sum, SECOND_COST
    )
    weight_grad = sum_blocks(weight_chips)
    query_grads, gate_total = pick_rows(
        target, first_returned, second_returned, row_grads.shape[0] // count
    )
    gate_value = jnp.tanh(gate_logit[0])
    gate_grad = (1.0 - gate_value * gate_value) * gate_total[0, 0]
    return query_grads, key_sum[None], value_sum[None], weight_grad, gate_grad.reshape(1)


def solution(mesh):
    in_specs = (
        P("rec", "ctx", None),
        P("rec", "ctx", None),
        P("rec", "ctx", None),
        P(),
        P(),
        P(("ctx", "rec"), None),
        P(("ctx", "rec")),
        P(("ctx", "rec")),
        P(("ctx", "rec")),
    )
    out_specs = (
        P(("ctx", "rec"), None),
        P("rec", "ctx", None),
        P("rec", "ctx", None),
        P(("ctx", "rec"), None),
        P(),
    )
    return jax.shard_map(local, mesh=mesh, in_specs=in_specs, out_specs=out_specs, check_vma=False)
```
